512 devices in a mesh: dp: 128 (over z, y, core), segment: 4 (over x).
Axes of the slice: x: 4, y: 8, z: 8, core: 2. Of those that a mesh axis runs over, the one named last changes fastest.
Arguments:
- images: bfloat16 [512, 16, 16, 384], P('dp'), may hold values from -6 to 6
- cotangent: bfloat16 [512, 16, 16, 384], P('dp'), may hold values from -0.0625 to 0.0625
- kernels: float32 [4, 49, 384], P('segment'), may hold values from -0.875 to 0.875
- norm_gains: float32 [4, 384], P('segment'), may hold values from 0.25 to 1.75
- w_in: bfloat16 [4, 384, 768], P('segment'), may hold values from -0.3125 to 0.3125
- w_out: bfloat16 [4, 768, 384], P('segment'), may hold values from -0.21875 to 0.21875
- scales: float32 [4, 384], P('segment'), may hold values from 0.3 to 1
Outputs:
- grad_kernels: float32 [4, 49, 384], P('segment', None, 'dp')
- grad_gains: float32 [4, 384], P('segment', 'dp')
- grad_w_in: float32 [4, 384, 768], P('segment', 'dp')
- grad_w_out: float32 [4, 768, 384], P('segment', None, 'dp')
- grad_scales: float32 [4, 384], P('segment', 'dp')
The draws below stay inside these ranges and needn't reach their ends.
All inputs are finite; a program needn't handle non-finite values.
Results may differ from the reference program's by a relative error of at most 0.034.
Values may be sent and summed in bfloat16 or wider, within the bound.
A program may use at most 64 MiB of HBM per device.

```python
import math
import jax
import jax.numpy as jnp
from jax import lax

C = 384
FF = 768
HH = 16
WW = 16
IMAGES = 512
N_SEGMENT = 4


def strengthened(values, key, source, target, shards_of, factor):
    def block_of(position):
        return (jnp.arange(values.shape[position]) // (values.shape[position] // shards_of)).reshape((-1,) + (1,) * (values.ndim - 1 - position))

    one_side = jax.random.permutation(key, shards_of)[block_of(target)]
    second = (block_of(target) + shards_of // 2) % shards_of
    return jnp.where((block_of(source) == one_side) | (block_of(source) == second), factor * values, values)


def shard_levels(stream_key, dims, split, least, high):
    def one(dim, blocks):
        heights = jax.random.uniform(jax.random.fold_in(jax.random.fold_in(stream_key, 6), dim), (blocks,), jnp.float32, least / len(split), high / len(split))
        return jnp.repeat(jnp.exp(heights), dims[dim] // blocks).reshape((-1,) + (1,) * (len(dims) - dim - 1))

    loudness = one(*split[0])
    for cut in split[1:]:
        loudness = loudness * one(*cut)
    return loudness


def centred(key, extent, scale, most, cuts=(), kind=jnp.bfloat16):
    factor_of = shard_levels(key, extent, cuts, -0.22, 0.18) if cuts else 1.0
    array = jax.random.normal(key, extent, jnp.float32) * scale * factor_of
    return jnp.minimum(jnp.maximum(array, -most), most).astype(kind)


def bell_draw_with(rng, dims, width, most, split, heavy, dtype=jnp.bfloat16):
    entries = width * jax.random.normal(rng, dims, jnp.float32)
    if split:
        entries = entries * shard_levels(rng, dims, split, -0.22, 0.18)
    return jnp.clip(strengthened(entries, jax.random.fold_in(rng, 3), *heavy), -most, most).astype(dtype)


def setup_inputs(seed: int = 0) -> dict:
    keys = jax.random.split(jax.random.key(seed), 8)
    return {
        "images": centred(keys[0], (IMAGES, HH, WW, C), 1.0, 6.0, ((0, 128),)),
        "cotangent": bell_draw_with(keys[1], (IMAGES, HH, WW, C), ((IMAGES * HH * WW) ** -0.5), 0.0625, ((0, 128),), (0, 3, 128, 5.5)),
        "kernels": centred(keys[2], (N_SEGMENT, 49, C), 49 ** -0.5, 0.875, ((0, 4),), jnp.float32),
        "norm_gains": jnp.clip(1.0 + 0.15 * jax.random.normal(keys[3], (N_SEGMENT, C), jnp.float32), 0.25, 1.75),
        "w_in": centred(keys[4], (N_SEGMENT, C, FF), C ** -0.5, 0.3125, ((0, 4),)),
        "w_out": centred(keys[5], (N_SEGMENT, FF, C), FF ** -0.5, 0.21875, ((0, 4),)),
        "scales": jnp.clip(jnp.exp(math.log(1.0) - 1.2039728 * jax.random.uniform(keys[6], (N_SEGMENT, C), jnp.float32) ** shard_levels(keys[6], (N_SEGMENT, C), ((0, 4),), -0.2, 0.2)), 0.3, 1.0),
    }


EPS = 1e-06

def depthwise(padded, kernel, map_rows, map_cols):
    running = jnp.zeros((padded.shape[0], map_rows, map_cols, padded.shape[3]), jnp.float32)
    for tap_row in range(7):
        for tap_col in range(7):
            running = running + kernel[tap_row * 7 + tap_col] * padded[:, tap_row:tap_row + map_rows, tap_col:tap_col + map_cols, :]
    return running

def forward_parts(inputs, kernel, layernorm_gain_vector, w_in, w_out, layer_scale):
    map_rows, map_cols, channels = (inputs.shape[1], inputs.shape[2], inputs.shape[3])
    padded = jnp.pad(inputs.astype(jnp.float32), ((0, 0), (3, 3), (3, 3), (0, 0)))
    conv_out = depthwise(padded, kernel, map_rows, map_cols)
    flat_rows = conv_out.reshape(-1, channels)
    center = flat_rows - lax.optimization_barrier(jnp.mean(flat_rows, axis=1, keepdims=True))
    inverse_deviation = lax.rsqrt(lax.optimization_barrier(jnp.mean(center * center, axis=1, keepdims=True)) + EPS)
    normalized_map = center * inverse_deviation
    normed_low = (normalized_map * layernorm_gain_vector).astype(jnp.bfloat16)
    pre_gelu = jnp.dot(normed_low, w_in, preferred_element_type=jnp.float32)
    hidden = jax.nn.gelu(pre_gelu).astype(jnp.bfloat16)
    branch = jnp.dot(hidden, w_out, preferred_element_type=jnp.float32)
    residual = inputs.astype(jnp.float32).reshape(flat_rows.shape)
    result = (residual + layer_scale * branch).astype(jnp.bfloat16).reshape(inputs.shape)
    return (result, (padded, normalized_map, inverse_deviation, normed_low, pre_gelu, hidden, branch))

def backward_parts(grad_map, stored, kernel, layernorm_gain_vector, w_in, w_out, layer_scale):
    padded, normalized_map, inverse_deviation, normed_low, pre_gelu, hidden, branch = stored
    grid_shape = grad_map.shape
    map_rows, map_cols, channels = (grid_shape[1], grid_shape[2], grid_shape[3])
    grad_out = grad_map.astype(jnp.float32).reshape(-1, channels)
    grad_scale = lax.optimization_barrier(jnp.sum(grad_out * branch, axis=0))
    grad_branch = (grad_out * layer_scale).astype(jnp.bfloat16)
    grad_wout = jnp.dot(hidden.T, grad_branch, preferred_element_type=jnp.float32)
    grad_hidden = jnp.dot(grad_branch, w_out.T, preferred_element_type=jnp.float32)
    grad_pre = jax.vjp(jax.nn.gelu, pre_gelu)[1](grad_hidden)[0].astype(jnp.bfloat16)
    grad_win = jnp.dot(normed_low.T, grad_pre, preferred_element_type=jnp.float32)
    normalized_map_gradient = jnp.dot(grad_pre, w_in.T, preferred_element_type=jnp.float32)
    grad_gain = lax.optimization_barrier(jnp.sum(normalized_map_gradient * normalized_map, axis=0))
    standardized_input_gradient = normalized_map_gradient * layernorm_gain_vector
    depthwise_output_gradient = inverse_deviation * (standardized_input_gradient - lax.optimization_barrier(jnp.mean(standardized_input_gradient, axis=1, keepdims=True)) - normalized_map * lax.optimization_barrier(jnp.mean(standardized_input_gradient * normalized_map, axis=1, keepdims=True)))
    depthwise_output_gradient = depthwise_output_gradient.reshape(grid_shape)
    grad_padded = jnp.pad(depthwise_output_gradient, ((0, 0), (3, 3), (3, 3), (0, 0)))
    grad_input = grad_out.reshape(grid_shape)
    kernel_rows = []
    for tap_row in range(7):
        for tap_col in range(7):
            window = padded[:, tap_row:tap_row + map_rows, tap_col:tap_col + map_cols, :]
            kernel_rows.append(lax.optimization_barrier(jnp.sum(window * depthwise_output_gradient, axis=(0, 1, 2))))
            grad_input = grad_input + kernel[tap_row * 7 + tap_col] * grad_padded[:, 6 - tap_row:6 - tap_row + map_rows, 6 - tap_col:6 - tap_col + map_cols, :]
    grad_kernel = jnp.stack(kernel_rows)
    return (grad_input.astype(jnp.bfloat16), (grad_kernel, grad_gain, grad_win, grad_wout, grad_scale))

def stack_member(results, member):
    return jnp.stack([segment_grads[member] for segment_grads in results])

def reference(images, cotangent, kernels, norm_gains, w_in, w_out, scales):
    segment_inputs = [images]
    for relay_segment_index in range(N_SEGMENT - 1):
        block_params = (kernels[relay_segment_index], norm_gains[relay_segment_index], w_in[relay_segment_index], w_out[relay_segment_index], scales[relay_segment_index])

        def advance(single, block_params=block_params):
            return forward_parts(single[None], *block_params)[0][0]
        segment_inputs.append(lax.map(advance, segment_inputs[-1]))
    channels = images.shape[3]
    hidden_units = w_in.shape[2]
    flowing = cotangent
    results = []
    for relay_segment_index in range(N_SEGMENT - 1, -1, -1):
        block_params = (kernels[relay_segment_index], norm_gains[relay_segment_index], w_in[relay_segment_index], w_out[relay_segment_index], scales[relay_segment_index])

        def accumulate(running, step_pair, block_params=block_params):
            single, grad_single = step_pair
            stored = forward_parts(single[None], *block_params)[1]
            grad_input, grad_terms = backward_parts(grad_single[None], stored, *block_params)
            return (jax.tree.map(jnp.add, running, grad_terms), grad_input[0])
        zero_terms = (jnp.zeros((49, channels), jnp.float32), jnp.zeros((channels,), jnp.float32), jnp.zeros((channels, hidden_units), jnp.float32), jnp.zeros((hidden_units, channels), jnp.float32), jnp.zeros((channels,), jnp.float32))
        running, flowing = lax.scan(accumulate, zero_terms, (segment_inputs[relay_segment_index], flowing))
        results.insert(0, running)
    return (stack_member(results, 0), stack_member(results, 1), stack_member(results, 2), stack_member(results, 3), stack_member(results, 4))
```

```python
import math

import jax
import jax.numpy as jnp
from jax import lax
from jax.experimental import pallas as pl
from jax.experimental.pallas import tpu as pltpu
from jax.sharding import PartitionSpec as P

EPS = 1e-06
LANES = 128
PAD = 8
GELU_A = math.sqrt(2.0 / math.pi)
GELU_B = 0.044715
F32 = jnp.float32
BF16 = jnp.bfloat16


def product(a, b):
    return jnp.dot(a, b, preferred_element_type=F32)


def product_nt(a, b):
    return lax.dot_general(a, b, (((1,), (1,)), ((), ())), preferred_element_type=F32)


def block_kernel(
    which,
    image_ref,
    cot_ref,
    small_ref,
    w_in_ref,
    w_out_ref,
    out_ref,
    xpad,
    gpad,
    current,
    conv,
    xhat,
    rstd,
    normed,
    hidden,
    slope,
    branch,
    wide,
    narrow,
    g_branch,
    g_pre,
    sums,
    order,
):
    blocks, channels, units = w_in_ref.shape
    rows, cols = image_ref.shape[1], image_ref.shape[2]
    positions = rows * cols
    chunks = channels // LANES
    tile = 2 * cols
    n_tiles = positions // tile

    def lanes(c):
        return slice(c * LANES, (c + 1) * LANES)

    r_i = lax.broadcasted_iota(jnp.int32, (channels, channels), 0)
    c_i = lax.broadcasted_iota(jnp.int32, (channels, channels), 1)
    group = channels // LANES
    order[...] = jnp.where(c_i == group * (r_i % LANES) + r_i // LANES, 1.0, 0.0).astype(BF16)

    xpad[...] = jnp.zeros_like(xpad)
    gpad[...] = jnp.zeros_like(gpad)
    current[...] = image_ref[0].reshape(positions, channels).astype(F32)

    def spread(ref, lead, p):
        for c in range(chunks):
            pass

    def taps(s, c, q):
        return [
            jnp.broadcast_to(
                small_ref[s, pl.ds(7 * r + q, 1), pl.ds(pl.multiple_of(c * LANES, LANES), LANES)],
                (8, LANES),
            )
            for r in range(7)
        ]

    def forward(s, carry):
        def store_row(i, carry):
            for c in range(chunks):
                xpad[s, c, i, PAD : PAD + cols, :] = current[
                    pl.ds(pl.multiple_of(i * cols, cols), cols), lanes(c)
                ]
            return carry

        lax.fori_loop(0, rows, store_row, 0)

        def conv_chunk(c, carry):
            acc = [[None, None] for _ in range(rows)]
            for q in range(7):
                weights = taps(s, c, q)
                for i in range(rows):
                    for half in range(cols // 8):
                        value = xpad[s, c, i, PAD - 3 + q + 8 * half : PAD + 5 + q + 8 * half, :]
                        for r in range(7):
                            o = i - r + 3
                            if 0 <= o < rows:
                                term = weights[r] * value
                                old = acc[o][half]
                                acc[o][half] = term if old is None else old + term
            for o in range(rows):
                for half in range(cols // 8):
                    conv[c, o * cols + 8 * half : o * cols + 8 * half + 8, :] = acc[o][half]
            return carry

        lax.fori_loop(0, chunks, conv_chunk, 0)

        gain = small_ref[s, 49:50, :]
        scale = small_ref[s, 50:51, :]

        def norm_tile(t, carry):
            at = pl.ds(pl.multiple_of(t * tile, tile), tile)
            parts = [conv[c, at, :] for c in range(chunks)]
            mean = jnp.sum(sum(parts), axis=1, keepdims=True) * (1.0 / channels)
            parts = [p - mean for p in parts]
            var = jnp.sum(sum(p * p for p in parts), axis=1, keepdims=True) * (1.0 / channels)
            inverse = lax.rsqrt(var + EPS)
            rstd[s, at, :] = jnp.broadcast_to(inverse, (tile, LANES))
            for c in range(chunks):
                value = parts[c] * inverse
                xhat[s, at, lanes(c)] = value
                normed[s, at, lanes(c)] = (value * gain[:, lanes(c)]).astype(BF16)
            return carry

        lax.fori_loop(0, n_tiles, norm_tile, 0)
        wide[...] = product(normed[s], w_in_ref[s])

        def gelu_tile(t, carry):
            at = pl.ds(pl.multiple_of(t * 16, 16), 16)
            value = wide[at, :]
            square = value * value
            gate = jnp.tanh(GELU_A * value * (1.0 + GELU_B * square))
            half = 0.5 * (1.0 + gate)
            hidden[s, at, :] = (value * half).astype(BF16)
            slope[s, at, :] = half + (0.5 * GELU_A) * value * (1.0 - gate * gate) * (
                1.0 + (3.0 * GELU_B) * square
            )
            return carry

        lax.fori_loop(0, positions // 16, gelu_tile, 0)
        branch[s] = product(hidden[s], w_out_ref[s])

        def residual_tile(t, carry):
            at = pl.ds(pl.multiple_of(t * tile, tile), tile)
            current[at, :] = current[at, :] + scale * branch[s, at, :]
            return carry

        lax.fori_loop(0, n_tiles, residual_tile, 0)
        return carry

    lax.fori_loop(0, blocks, forward, 0)
    current[...] = cot_ref[0].reshape(positions, channels).astype(F32)
    sums[...] = jnp.zeros_like(sums)

    def backward(step, carry):
        s = blocks - 1 - step
        gain = small_ref[s, 49:50, :]
        scale = small_ref[s, 50:51, :]

        def scale_tile(t, total):
            at = pl.ds(pl.multiple_of(t * tile, tile), tile)
            value = current[at, :]
            g_branch[at, :] = (value * scale).astype(BF16)
            return total + jnp.sum((value * branch[s, at, :]).reshape(tile // 8, 8, channels), axis=0)

        total = lax.fori_loop(0, n_tiles, scale_tile, jnp.zeros((8, channels), F32))
        sums[50:51, :] = jnp.sum(total, axis=0, keepdims=True)
        wide[...] = product_nt(g_branch[...], w_out_ref[s])

        def slope_tile(t, carry):
            at = pl.ds(pl.multiple_of(t * 16, 16), 16)
            g_pre[at, :] = (wide[at, :] * slope[s, at, :]).astype(BF16)
            return carry

        lax.fori_loop(0, positions // 16, slope_tile, 0)
        narrow[...] = product_nt(g_pre[...], w_in_ref[s])
        turned = product_nt(order[...], normed[s]).astype(BF16)
        out_ref[s, :, :units] = product(turned, g_pre[...]).astype(out_ref.dtype)
        turned = product_nt(order[...], g_branch[...]).astype(BF16)
        out_ref[s, :, units : 2 * units] = product(turned, hidden[s]).astype(out_ref.dtype)

        def norm_row(i, total):
            at = pl.ds(pl.multiple_of(i * cols, cols), cols)
            grad = narrow[at, :]
            hat = xhat[s, at, :]
            both = grad * hat
            total = total + jnp.sum(both.reshape(cols // 8, 8, channels), axis=0)
            grad = grad * gain
            both = both * gain
            mean = jnp.sum(
                sum(grad[:, lanes(c)] for c in range(chunks)), axis=1, keepdims=True
            ) * (1.0 / channels)
            cross = jnp.sum(
                sum(both[:, lanes(c)] for c in range(chunks)), axis=1, keepdims=True
            ) * (1.0 / channels)
            inverse = rstd[s, at, :]
            for c in range(chunks):
                gpad[c, i, PAD : PAD + cols, :] = inverse * (
                    grad[:, lanes(c)] - mean - hat[:, lanes(c)] * cross
                )
            return total

        total = lax.fori_loop(0, rows, norm_row, jnp.zeros((8, channels), F32))
        sums[49:50, :] = jnp.sum(total, axis=0, keepdims=True)

        def conv_chunk(c, carry):
            at_c = pl.ds(pl.multiple_of(c * LANES, LANES), LANES)
            acc = [[None, None] for _ in range(rows)]
            for q in range(7):
                weights = taps(s, c, q)
                for i in range(rows):
                    for half in range(cols // 8):
                        start = PAD + 3 - q + 8 * half
                        value = gpad[c, i, start : start + 8, :]
                        for r in range(7):
                            o = i + r - 3
                            if 0 <= o < rows:
                                term = weights[r] * value
                                old = acc[o][half]
                                acc[o][half] = term if old is None else old + term
            for o in range(rows):
                for half in range(cols // 8):
                    at = slice(o * cols + 8 * half, o * cols + 8 * half + 8)
                    current[at, at_c] = current[at, at_c] + acc[o][half]
            return carry

        lax.fori_loop(0, chunks, conv_chunk, 0)

        def kernel_chunk(c, carry):
            at_c = pl.ds(pl.multiple_of(c * LANES, LANES), LANES)
            grads = [
                [gpad[c, o, PAD + 8 * half : PAD + 8 * half + 8, :] for half in range(cols // 8)]
                for o in range(rows)
            ]
            for q in range(7):
                acc = [None] * 7
                for i in range(rows):
                    for half in range(cols // 8):
                        value = xpad[s, c, i, PAD - 3 + q + 8 * half : PAD + 5 + q + 8 * half, :]
                        for r in range(7):
                            o = i - r + 3
                            if 0 <= o < rows:
                                term = grads[o][half] * value
                                acc[r] = term if acc[r] is None else acc[r] + term
                for r in range(7):
                    sums[7 * r + q : 7 * r + q + 1, at_c] = jnp.sum(acc[r], axis=0, keepdims=True)
            return carry

        lax.fori_loop(0, chunks, kernel_chunk, 0)
        out_ref[s, :, 2 * units :] = product_nt(order[...], sums[...].astype(BF16)).astype(
            out_ref.dtype
        )
        return carry

    lax.fori_loop(0, blocks, backward, 0)


def block_terms(which, images, cotangent, small, w_in, w_out, dtype):
    blocks, channels, units = w_in.shape
    rows, cols = images.shape[1:3]
    positions = rows * cols
    chunks = channels // LANES
    whole = lambda *shape: pl.BlockSpec(shape, lambda i, w: (0,) * len(shape))
    one = pl.BlockSpec((1, rows, cols, channels), lambda i, w: (w[0], 0, 0, 0))
    out = (blocks, channels, 2 * units + LANES)
    return pl.pallas_call(
        block_kernel,
        out_shape=jax.ShapeDtypeStruct(out, dtype),
        grid_spec=pltpu.PrefetchScalarGridSpec(
            num_scalar_prefetch=1,
            grid=(1,),
            in_specs=[one, one, whole(*small.shape), whole(*w_in.shape), whole(*w_out.shape)],
            out_specs=whole(*out),
            scratch_shapes=[
                pltpu.VMEM((blocks, chunks, rows, cols + 2 * PAD, LANES), F32),
                pltpu.VMEM((chunks, rows, cols + 2 * PAD, LANES), F32),
                pltpu.VMEM((positions, channels), F32),
                pltpu.VMEM((chunks, positions, LANES), F32),
                pltpu.VMEM((blocks, positions, channels), F32),
                pltpu.VMEM((blocks, positions, LANES), F32),
                pltpu.VMEM((blocks, positions, channels), BF16),
                pltpu.VMEM((blocks, positions, units), BF16),
                pltpu.VMEM((blocks, positions, units), F32),
                pltpu.VMEM((blocks, positions, channels), F32),
                pltpu.VMEM((positions, units), F32),
                pltpu.VMEM((positions, channels), F32),
                pltpu.VMEM((positions, channels), BF16),
                pltpu.VMEM((positions, units), BF16),
                pltpu.VMEM((LANES, channels), F32),
                pltpu.VMEM((channels, channels), BF16),
            ],
        ),
        compiler_params=pltpu.CompilerParams(vmem_limit_bytes=60 * 1024 * 1024),
        name="blocks",
    )(which, images, cotangent, small, w_in, w_out)


def local(images, cotangent, kernels, norm_gains, w_in, w_out, scales):
    channels, units = w_in.shape[1:]
    which = lax.axis_index("segment").astype(jnp.int32)[None]
    small = jnp.concatenate([kernels, norm_gains[:, None], scales[:, None]], axis=1)
    small = jnp.pad(small, ((0, 0), (0, 56 - small.shape[1]), (0, 0)))
    small = lax.all_gather(small, "segment", axis=0, tiled=True)
    w_in = lax.all_gather(w_in, "segment", axis=0, tiled=True)
    w_out = lax.all_gather(w_out, "segment", axis=0, tiled=True)
    terms = block_terms(which, images, cotangent, small, w_in, w_out, F32)
    terms = lax.psum_scatter(terms, "segment", scatter_dimension=0, tiled=True)
    terms = terms.reshape(channels // LANES, LANES, terms.shape[-1])
    terms = lax.psum_scatter(terms, "dp", scatter_dimension=1, tiled=True)[:, 0]
    return (
        terms[:, 2 * units : 2 * units + 49].T[None],
        terms[:, 2 * units + 49][None],
        terms[:, :units][None],
        terms[:, units : 2 * units].T[None],
        terms[:, 2 * units + 50][None],
    )


def solution(mesh):
    in_specs = (
        P("dp", None, None, None),
        P("dp", None, None, None),
        P("segment", None, None),
        P("segment", None),
        P("segment", None, None),
        P("segment", None, None),
        P("segment", None),
    )
    out_specs = (
        P("segment", None, "dp"),
        P("segment", "dp"),
        P("segment", "dp", None),
        P("segment", None, "dp"),
        P("segment", "dp"),
    )
    return jax.shard_map(local, mesh=mesh, in_specs=in_specs, out_specs=out_specs, check_vma=False)
```

```python
import math

import jax
import jax.numpy as jnp
import numpy as np
from jax import lax
from jax.experimental import pallas as pl
from jax.experimental.pallas import tpu as pltpu
from jax.sharding import PartitionSpec as P

EPS = 1e-06
LANES = 128
PAD = 8
GELU_A = math.sqrt(2.0 / math.pi)
GELU_B = 0.044715
F32 = jnp.float32
BF16 = jnp.bfloat16
NX, NY, NZ, NC = 4, 8, 8, 2
MESH = pl.DeviceIdType.MESH


def product(a, b):
    return jnp.dot(a, b, preferred_element_type=F32)


def product_nt(a, b):
    return lax.dot_general(a, b, (((1,), (1,)), ((), ())), preferred_element_type=F32)


def send_orders(channels):
    each = channels // (NZ * NY * NC)
    number = np.arange(channels).reshape(NZ, NY, NC, each)
    rows = [number.transpose(2, 0, 1, 3).reshape(-1), number.transpose(2, 1, 0, 3).reshape(-1)]
    return np.stack([np.eye(channels, dtype=np.float32)[r] for r in rows])


def block_kernel(
    images_ref,
    cot_ref,
    kernels_ref,
    gains_ref,
    scales_ref,
    w_in_ref,
    w_out_ref,
    order_ref,
    grad_in_ref,
    grad_out_ref,
    grad_small_ref,
    image,
    cot,
    small_all,
    w_in_all,
    w_out_all,
    xpad,
    gpad,
    current,
    conv,
    xhat,
    rstd,
    normed,
    hidden,
    slope,
    branch,
    wide,
    narrow,
    g_branch,
    g_pre,
    sums,
    stage_in,
    stage_out,
    stage_small,
    half_in,
    half_out,
    half_small,
    got_in,
    got_out,
    got_small,
    flat_in,
    flat_out,
    flat_small,
    cut_in,
    cut_out,
    part_in,
    part_out,
    total_in,
    total_out,
    last_in,
    last_out,
    local_sem,
    small_send,
    small_recv,
    wi_send,
    wi_recv,
    wo_send,
    wo_recv,
    ci_send,
    ci_recv,
    co_send,
    co_recv,
    a_send,
    a_recv,
    b_send,
    b_recv,
    c_send,
    c_recv,
    d_send,
    d_recv,
):
    blocks, channels, units = w_in_all.shape
    rows, cols = image.shape[0], image.shape[1]
    positions = rows * cols
    chunks = channels // LANES
    tile = 2 * cols
    n_tiles = positions // tile
    each = channels // (NZ * NY * NC)
    span = each * NY
    wide_half = units // 2

    me = lax.axis_index("segment")
    dp = lax.axis_index("dp")
    core = lax.rem(dp, NC)
    y = lax.rem(dp // NC, NY)
    z = dp // (NC * NY)
    mate = dp + 1 - 2 * core

    def device(z_to, y_to):
        return (z_to * NY + y_to) * NC + core

    def shifted(base, by, size):
        return lax.rem(base + by, size)

    def remote(src, dst, ssem, rsem, to_dp, to_x):
        return pltpu.make_async_remote_copy(
            src_ref=src,
            dst_ref=dst,
            send_sem=ssem,
            recv_sem=rsem,
            device_id=(to_dp, to_x),
            device_id_type=MESH,
        )

    def arrived(ref, sem):
        pltpu.make_async_copy(ref, ref, sem).wait()

    image_copy = pltpu.make_async_copy(images_ref.at[me], image, local_sem.at[0])
    cot_copy = pltpu.make_async_copy(cot_ref.at[me], cot, local_sem.at[1])
    in_copy = pltpu.make_async_copy(w_in_ref.at[0], w_in_all.at[me], local_sem.at[2])
    out_copy = pltpu.make_async_copy(w_out_ref.at[0], w_out_all.at[me], local_sem.at[3])
    for copy in (image_copy, cot_copy, in_copy, out_copy):
        copy.start()
    barrier = pltpu.get_barrier_semaphore()
    pl.semaphore_signal(barrier, inc=1, device_id=(mate, me), device_id_type=MESH)
    for k in range(1, NX):
        pl.semaphore_signal(
            barrier, inc=1, device_id=(dp, shifted(me, k, NX)), device_id_type=MESH
        )
    for k in range(1, NZ):
        pl.semaphore_signal(
            barrier, inc=1, device_id=(device(shifted(z, k, NZ), y), me), device_id_type=MESH
        )
    for k in range(1, NY):
        pl.semaphore_signal(
            barrier, inc=1, device_id=(device(z, shifted(y, k, NY)), me), device_id_type=MESH
        )
    small_all[me, 0:49, :] = kernels_ref[0]
    small_all[me, 49:50, :] = gains_ref[...]
    small_all[me, 50:51, :] = scales_ref[...]
    small_all[me, 51:56, :] = jnp.zeros((5, channels), F32)
    xpad[...] = jnp.zeros_like(xpad)
    gpad[...] = jnp.zeros_like(gpad)
    sums[...] = jnp.zeros_like(sums)
    pl.semaphore_wait(barrier, 1 + (NX - 1) + (NZ - 1) + (NY - 1))

    right, left = shifted(me, 1, NX), shifted(me, NX - 1, NX)
    in_rows = pl.ds(pl.multiple_of(core * (channels // 2), 64), channels // 2)
    out_rows = pl.ds(pl.multiple_of(core * (units // 2), 64), units // 2)

    def small_push(k):
        return remote(
            small_all.at[me],
            small_all.at[me],
            small_send.at[k - 1],
            small_recv.at[NX - k - 1],
            dp,
            shifted(me, k, NX),
        )

    def in_push(slot, k, src, shard, to_x):
        return remote(
            src, w_in_all.at[shard, in_rows], wi_send.at[slot], wi_recv.at[k - 1], dp, to_x
        )

    def out_push(slot, k, src, shard, to_x):
        return remote(
            src, w_out_all.at[shard, out_rows], wo_send.at[slot], wo_recv.at[k - 1], dp, to_x
        )

    in_own, out_own = w_in_ref.at[0, in_rows], w_out_ref.at[0, out_rows]
    pushes = [small_push(k) for k in range(1, NX)] + [
        in_push(0, 3, in_own, me, right),
        out_push(1, 1, out_own, me, left),
        in_push(1, 1, in_own, me, left),
        out_push(0, 3, out_own, me, right),
    ]
    for push in pushes:
        push.start()
    in_relay = in_push(2, 2, w_in_all.at[left, in_rows], left, right)
    out_relay = out_push(2, 2, w_out_all.at[right, out_rows], right, left)

    def in_mate(shard, k):
        part = w_in_all.at[shard, in_rows]
        return remote(part, part, ci_send.at[k - 1], ci_recv.at[k - 1], mate, me)

    def out_mate(shard, k):
        part = w_out_all.at[shard, out_rows]
        return remote(part, part, co_send.at[k - 1], co_recv.at[k - 1], mate, me)

    def relay():
        arrived(w_in_all.at[left, in_rows], wi_recv.at[2])
        in_relay.start()
        arrived(w_out_all.at[right, out_rows], wo_recv.at[0])
        out_relay.start()

    def arrive(shard):
        for k in range(1, NX):

            @pl.when(lax.rem(shard - me + NX, NX) == k)
            def _():
                if k != 3:
                    arrived(w_in_all.at[shard, in_rows], wi_recv.at[k - 1])
                in_mate(shard, k).start()
                if k != 1:
                    arrived(w_out_all.at[shard, out_rows], wo_recv.at[k - 1])
                out_mate(shard, k).start()

    def complete(shard):
        @pl.when(shard == me)
        def _():
            in_copy.wait()
            out_copy.wait()

        for k in range(1, NX):

            @pl.when(lax.rem(shard - me + NX, NX) == k)
            def _():
                arrived(w_in_all.at[shard, in_rows], ci_recv.at[k - 1])
                arrived(w_out_all.at[shard, out_rows], co_recv.at[k - 1])

    def a_copies(s):
        there = 1 - core
        return [
            remote(stage.at[s, there], half.at[s], a_send.at[s, p], a_recv.at[s, p], mate, me)
            for p, (stage, half) in enumerate(
                ((stage_in, half_in), (stage_out, half_out), (stage_small, half_small))
            )
        ]

    def b_copies(s):
        found = []
        for p, (half, got) in enumerate(
            ((half_in, got_in), (half_out, got_out), (half_small, got_small))
        ):
            for k in range(1, NZ):
                at = shifted(y if p == 1 else z, k, NZ)
                to = device(z, at) if p == 1 else device(at, y)
                found.append(
                    remote(
                        half.at[s, at], got.at[s, k - 1], b_send.at[s, p], b_recv.at[s, p], to, me
                    )
                )
        return found

    def c_copies(s):
        found = []
        for p, (cut, part) in enumerate(((cut_in, part_in), (cut_out, part_out))):
            for k in range(1, NZ):
                at = shifted(z if p == 1 else y, k, NZ)
                to = device(at, y) if p == 1 else device(z, at)
                found.append(
                    remote(
                        cut.at[s, at], part.at[s, k - 1], c_send.at[s, p], c_recv.at[s, p], to, me
                    )
                )
        return found

    def d_copies():
        found = []
        for p, (total, last) in enumerate(((total_in, last_in), (total_out, last_out))):
            for k in range(1, NX):
                at = shifted(me, k, NX)
                found.append(
                    remote(total.at[at], last.at[k - 1], d_send.at[p], d_recv.at[p], dp, at)
                )
        return found

    def pair_sum(s):
        for p, (stage, half) in enumerate(
            ((stage_in, half_in), (stage_out, half_out), (stage_small, half_small))
        ):
            arrived(half.at[s], a_recv.at[s, p])

            def add(i, carry):
                value = half[s, i].astype(F32) + stage[s, core, i].astype(F32)
                half[s, i] = value.astype(half.dtype)
                return carry

            lax.fori_loop(0, NZ, add, 0)
        for copy in b_copies(s):
            copy.start()

    def line_sum(s):
        for p, (half, got, flat) in enumerate(
            (
                (half_in, got_in, flat_in),
                (half_out, got_out, flat_out),
                (half_small, got_small, flat_small),
            )
        ):
            arrived(got.at[s], b_recv.at[s, p])
            value = half[s, y if p == 1 else z].astype(F32)
            for k in range(NZ - 1):
                value = value + got[s, k].astype(F32)
            flat[...] = value
        for i in range(NY):
            cut_in[s, i, 0:each, :wide_half] = flat_in[each * i : each * i + each, :]
            cut_in[s, i, each : 2 * each, :wide_half] = flat_in[
                span + each * i : span + each * i + each, :
            ]
            tail = flat_small[each * i : each * i + each, :]
            cut_in[s, i, 0:each, wide_half:] = tail
            cut_in[s, i, each : 2 * each, wide_half:] = tail
            cut_out[s, i, 0:each, :] = flat_out[each * i : each * i + each, :]
            cut_out[s, i, each : 2 * each, :] = flat_out[
                span + each * i : span + each * i + each, :
            ]
        for copy in c_copies(s):
            copy.start()

    def plane_sum(s):
        for p, (cut, part, total) in enumerate(
            ((cut_in, part_in, total_in), (cut_out, part_out, total_out))
        ):
            arrived(part.at[s], c_recv.at[s, p])
            value = cut[s, z if p == 1 else y]
            for k in range(NY - 1):
                value = value + part[s, k]
            total[s] = value

    def lanes(c):
        return slice(c * LANES, (c + 1) * LANES)

    def taps(s, c, q):
        return [
            small_all[s, pl.ds(7 * r + q, 1), pl.ds(pl.multiple_of(c * LANES, LANES), LANES)][None]
            for r in range(7)
        ]

    image_copy.wait()
    current[...] = image[...].reshape(positions, channels).astype(F32)
    for k in range(1, NX):
        arrived(small_all.at[me], small_recv.at[k - 1])

    def forward(s, carry):
        def store_row(i, carry):
            for c in range(chunks):
                xpad[s, c, i + 3, PAD : PAD + cols, :] = current[
                    pl.ds(pl.multiple_of(i * cols, cols), cols), lanes(c)
                ]
            return carry

        lax.fori_loop(0, rows, store_row, 0)

        def conv_chunk(c, carry):
            acc = jnp.zeros((rows, cols, LANES), F32)
            for q in range(7):
                weights = taps(s, c, q)
                for r in range(7):
                    acc = acc + weights[r] * xpad[s, c, r : r + rows, PAD - 3 + q : PAD - 3 + q + cols, :]
            conv[c] = acc.reshape(positions, LANES)
            return carry

        lax.fori_loop(0, chunks, conv_chunk, 0)

        gain = small_all[s, 49:50, :]
        scale = small_all[s, 50:51, :]

        def norm_tile(t, carry):
            at = pl.ds(pl.multiple_of(t * tile, tile), tile)
            parts = [conv[c, at, :] for c in range(chunks)]
            mean = jnp.sum(sum(parts), axis=1, keepdims=True) * (1.0 / channels)
            parts = [p - mean for p in parts]
            var = jnp.sum(sum(p * p for p in parts), axis=1, keepdims=True) * (1.0 / channels)
            inverse = lax.rsqrt(var + EPS)
            rstd[s, at, :] = jnp.broadcast_to(inverse, (tile, LANES))
            for c in range(chunks):
                value = parts[c] * inverse
                xhat[s, at, lanes(c)] = value
                normed[s, at, lanes(c)] = (value * gain[:, lanes(c)]).astype(BF16)
            return carry

        lax.fori_loop(0, n_tiles, norm_tile, 0, unroll=4)

        @pl.when(s == 0)
        def _():
            relay()
            arrive(s)

        complete(s)
        wide[...] = product(normed[s], w_in_all[s])

        def gelu_tile(t, carry):
            at = pl.ds(pl.multiple_of(t * 16, 16), 16)
            value = wide[at, :]
            square = value * value
            gate = jnp.tanh(GELU_A * value * (1.0 + GELU_B * square))
            half = 0.5 * (1.0 + gate)
            hidden[s, at, :] = (value * half).astype(BF16)
            slope[s, at, :] = half + (0.5 * GELU_A) * value * (1.0 - gate * gate) * (
                1.0 + (3.0 * GELU_B) * square
            )
            return carry

        lax.fori_loop(0, positions // 16, gelu_tile, 0)
        branch[s] = product(hidden[s], w_out_all[s])

        @pl.when(s < blocks - 1)
        def _():
            arrive(s + 1)

        def residual_tile(t, carry):
            at = pl.ds(pl.multiple_of(t * tile, tile), tile)
            current[at, :] = current[at, :] + scale * branch[s, at, :]
            return carry

        lax.fori_loop(0, n_tiles, residual_tile, 0)
        return carry

    lax.fori_loop(0, blocks, forward, 0)
    cot_copy.wait()
    current[...] = cot[...].reshape(positions, channels).astype(F32)

    def backward(step, carry):
        s = blocks - 1 - step
        gain = small_all[s, 49:50, :]
        scale = small_all[s, 50:51, :]

        def scale_tile(t, total):
            at = pl.ds(pl.multiple_of(t * tile, tile), tile)
            value = current[at, :]
            g_branch[at, :] = (value * scale).astype(BF16)
            return total + jnp.sum((value * branch[s, at, :]).reshape(tile // 8, 8, channels), axis=0)

        total = lax.fori_loop(0, n_tiles, scale_tile, jnp.zeros((8, channels), F32))
        sums[50:51, :] = jnp.sum(total, axis=0, keepdims=True)
        wide[...] = product_nt(g_branch[...], w_out_all[s])

        def slope_tile(t, carry):
            at = pl.ds(pl.multiple_of(t * 16, 16), 16)
            g_pre[at, :] = (wide[at, :] * slope[s, at, :]).astype(BF16)
            return carry

        lax.fori_loop(0, positions // 16, slope_tile, 0)
        narrow[...] = product_nt(g_pre[...], w_in_all[s])
        def staged(stage, order, kept, other):
            turned = product_nt(order_ref[order], kept).astype(BF16)
            for h in range(NC):
                lo = h * (channels // 2)
                value = product(turned[lo : lo + channels // 2], other)
                for i in range(NZ):
                    piece = value[i * span : (i + 1) * span]
                    stage[s, h, i] = jnp.concatenate(
                        [piece[:, :wide_half], piece[:, wide_half:]], axis=0
                    ).astype(BF16)

        staged(stage_in, 0, normed[s], g_pre[...])
        staged(stage_out, 1, g_branch[...], hidden[s])

        @pl.when(step >= 1)
        def _():
            pair_sum(s + 1)

        @pl.when(step >= 2)
        def _():
            plane_sum(s + 2)

        def norm_row(i, total):
            at = pl.ds(pl.multiple_of(i * cols, cols), cols)
            grad = narrow[at, :]
            hat = xhat[s, at, :]
            both = grad * hat
            total = total + jnp.sum(both.reshape(cols // 8, 8, channels), axis=0)
            grad = grad * gain
            both = both * gain
            mean = jnp.sum(
                sum(grad[:, lanes(c)] for c in range(chunks)), axis=1, keepdims=True
            ) * (1.0 / channels)
            cross = jnp.sum(
                sum(both[:, lanes(c)] for c in range(chunks)), axis=1, keepdims=True
            ) * (1.0 / channels)
            inverse = rstd[s, at, :]
            for c in range(chunks):
                gpad[c, i + 3, PAD : PAD + cols, :] = inverse * (
                    grad[:, lanes(c)] - mean - hat[:, lanes(c)] * cross
                )
            return total

        total = lax.fori_loop(0, rows, norm_row, jnp.zeros((8, channels), F32), unroll=4)
        sums[49:50, :] = jnp.sum(total, axis=0, keepdims=True)

        def conv_chunk(c, carry):
            at_c = pl.ds(pl.multiple_of(c * LANES, LANES), LANES)
            acc = jnp.zeros((rows, cols, LANES), F32)
            for q in range(7):
                weights = taps(s, c, q)
                for r in range(7):
                    acc = acc + weights[r] * gpad[c, 6 - r : 6 - r + rows, PAD + 3 - q : PAD + 3 - q + cols, :]
            current[:, at_c] = current[:, at_c] + acc.reshape(positions, LANES)
            return carry

        lax.fori_loop(0, chunks, conv_chunk, 0)

        def kernel_chunk(c, carry):
            at_c = pl.ds(pl.multiple_of(c * LANES, LANES), LANES)
            for q in range(7):
                for r in range(7):
                    both = gpad[c, 3 : 3 + rows, PAD : PAD + cols, :] * xpad[s, c, r : r + rows, PAD - 3 + q : PAD - 3 + q + cols, :]
                    sums[7 * r + q : 7 * r + q + 1, at_c] = jnp.sum(both.reshape(positions, LANES), axis=0, keepdims=True)
            return carry

        lax.fori_loop(0, chunks, kernel_chunk, 0)
        value = product_nt(order_ref[0], sums[...].astype(BF16))
        for h in range(NC):
            for i in range(NZ):
                lo = h * (channels // 2) + i * span
                stage_small[s, h, i] = value[lo : lo + span]
        for copy in a_copies(s):
            copy.start()

        @pl.when(step >= 1)
        def _():
            line_sum(s + 1)

        return carry

    lax.fori_loop(0, blocks, backward, 0)
    pair_sum(0)
    plane_sum(1)
    line_sum(0)
    plane_sum(0)
    last = d_copies()
    for copy in last:
        copy.start()
    for p, (total, tail) in enumerate(((total_in, last_in), (total_out, last_out))):
        arrived(tail, d_recv.at[p])
        value = total[me]
        for k in range(NX - 1):
            value = value + tail[k]
        ref = grad_out_ref if p == 1 else grad_in_ref
        ref[:, :wide_half] = value[0:each, :wide_half]
        ref[:, wide_half:] = value[each : 2 * each, :wide_half]
        if p == 0:
            grad_small_ref[...] = value[0:each, wide_half:]

    for copy in pushes + [in_relay, out_relay] + last:
        copy.wait_send()
    for k in range(1, NX):
        shard = shifted(me, k, NX)
        in_mate(shard, k).wait_send()
        out_mate(shard, k).wait_send()

    def drain(s, carry):
        for copy in a_copies(s) + b_copies(s) + c_copies(s):
            copy.wait_send()
        return carry

    lax.fori_loop(0, blocks, drain, 0)


def local(images, cotangent, kernels, norm_gains, w_in, w_out, scales):
    channels, units = w_in.shape[1:]
    rows, cols = images.shape[1:3]
    positions = rows * cols
    blocks = NX
    chunks = channels // LANES
    each = channels // (NZ * NY * NC)
    span = each * NY
    wide_half = units // 2
    orders = jnp.asarray(send_orders(channels), BF16)
    vmem = pl.BlockSpec(memory_space=pltpu.VMEM)
    anywhere = pl.BlockSpec(memory_space=pl.ANY)
    dma = pltpu.SemaphoreType.DMA
    grad_in, grad_out, grad_small = pl.pallas_call(
        block_kernel,
        out_shape=[
            jax.ShapeDtypeStruct((each, units), F32),
            jax.ShapeDtypeStruct((each, units), F32),
            jax.ShapeDtypeStruct((each, LANES), F32),
        ],
        in_specs=[anywhere, anywhere, vmem, vmem, vmem, anywhere, anywhere, vmem],
        out_specs=[vmem, vmem, vmem],
        scratch_shapes=[
            pltpu.VMEM((rows, cols, channels), BF16),
            pltpu.VMEM((rows, cols, channels), BF16),
            pltpu.VMEM((blocks, 56, channels), F32),
            pltpu.VMEM((blocks, channels, units), BF16),
            pltpu.VMEM((blocks, units, channels), BF16),
            pltpu.VMEM((blocks, chunks, rows + 6, cols + 2 * PAD, LANES), F32),
            pltpu.VMEM((chunks, rows + 6, cols + 2 * PAD, LANES), F32),
            pltpu.VMEM((positions, channels), F32),
            pltpu.VMEM((chunks, positions, LANES), F32),
            pltpu.VMEM((blocks, positions, channels), F32),
            pltpu.VMEM((blocks, positions, LANES), F32),
            pltpu.VMEM((blocks, positions, channels), BF16),
            pltpu.VMEM((blocks, positions, units), BF16),
            pltpu.VMEM((blocks, positions, units), F32),
            pltpu.VMEM((blocks, positions, channels), F32),
            pltpu.VMEM((positions, units), F32),
            pltpu.VMEM((positions, channels), F32),
            pltpu.VMEM((positions, channels), BF16),
            pltpu.VMEM((positions, units), BF16),
            pltpu.VMEM((LANES, channels), F32),
            pltpu.VMEM((blocks, NC, NZ, 2 * span, wide_half), BF16),
            pltpu.VMEM((blocks, NC, NZ, 2 * span, wide_half), BF16),
            pltpu.VMEM((blocks, NC, NZ, span, LANES), F32),
            pltpu.VMEM((blocks, NZ, 2 * span, wide_half), BF16),
            pltpu.VMEM((blocks, NZ, 2 * span, wide_half), BF16),
            pltpu.VMEM((blocks, NZ, span, LANES), F32),
            pltpu.VMEM((blocks, NZ - 1, 2 * span, wide_half), BF16),
            pltpu.VMEM((blocks, NZ - 1, 2 * span, wide_half), BF16),
            pltpu.VMEM((blocks, NZ - 1, span, LANES), F32),
            pltpu.VMEM((2 * span, wide_half), F32),
            pltpu.VMEM((2 * span, wide_half), F32),
            pltpu.VMEM((span, LANES), F32),
            pltpu.VMEM((blocks, NY, 2 * each, wide_half + LANES), F32),
            pltpu.VMEM((blocks, NY, 2 * each, wide_half), F32),
            pltpu.VMEM((blocks, NY - 1, 2 * each, wide_half + LANES), F32),
            pltpu.VMEM((blocks, NY - 1, 2 * each, wide_half), F32),
            pltpu.VMEM((blocks, 2 * each, wide_half + LANES), F32),
            pltpu.VMEM((blocks, 2 * each, wide_half), F32),
            pltpu.VMEM((NX - 1, 2 * each, wide_half + LANES), F32),
            pltpu.VMEM((NX - 1, 2 * each, wide_half), F32),
            dma((4,)),
            dma((NX - 1,)),
            dma((NX - 1,)),
            dma((3,)),
            dma((NX - 1,)),
            dma((3,)),
            dma((NX - 1,)),
            dma((NX - 1,)),
            dma((NX - 1,)),
            dma((NX - 1,)),
            dma((NX - 1,)),
            dma((blocks, 3)),
            dma((blocks, 3)),
            dma((blocks, 3)),
            dma((blocks, 3)),
            dma((blocks, 2)),
            dma((blocks, 2)),
            dma((2,)),
            dma((2,)),
        ],
        compiler_params=pltpu.CompilerParams(
            vmem_limit_bytes=60 * 1024 * 1024, collective_id=0, has_side_effects=True
        ),
        name="blocks",
    )(images, cotangent, kernels, norm_gains, scales, w_in, w_out, orders)
    return (
        grad_small[:, :49].T[None],
        grad_small[:, 49][None],
        grad_in[None],
        grad_out.T[None],
        grad_small[:, 50][None],
    )


def solution(mesh):
    in_specs = (
        P("dp", None, None, None),
        P("dp", None, None, None),
        P("segment", None, None),
        P("segment", None),
        P("segment", None, None),
        P("segment", None, None),
        P("segment", None),
    )
    out_specs = (
        P("segment", None, "dp"),
        P("segment", "dp"),
        P("segment", "dp", None),
        P("segment", None, "dp"),
        P("segment", "dp"),
    )
    return jax.shard_map(local, mesh=mesh, in_specs=in_specs, out_specs=out_specs, check_vma=False)
```

```python
import math

import jax
import jax.numpy as jnp
import numpy as np
from jax import lax
from jax.experimental import pallas as pl
from jax.experimental.pallas import tpu as pltpu
from jax.sharding import PartitionSpec as P

EPS = 1e-06
LANES = 128
PAD = 8
GELU_A = math.sqrt(2.0 / math.pi)
GELU_B = 0.044715
F32 = jnp.float32
BF16 = jnp.bfloat16
NX, NY, NZ, NC = 4, 8, 8, 2
MESH = pl.DeviceIdType.MESH


def product(a, b):
    return jnp.dot(a, b, preferred_element_type=F32)


def product_nt(a, b):
    return lax.dot_general(a, b, (((1,), (1,)), ((), ())), preferred_element_type=F32)


def send_orders(channels):
    each = channels // (NZ * NY * NC)
    number = np.arange(channels).reshape(NZ, NY, NC, each)
    rows = [number.transpose(2, 0, 1, 3).reshape(-1), number.transpose(2, 1, 0, 3).reshape(-1)]
    return np.stack([np.eye(channels, dtype=np.float32)[r] for r in rows])


def block_kernel(
    images_ref,
    cot_ref,
    kernels_ref,
    gains_ref,
    scales_ref,
    w_in_ref,
    w_out_ref,
    order_ref,
    grad_in_ref,
    grad_out_ref,
    grad_kernel_ref,
    grad_gain_ref,
    grad_scale_ref,
    image,
    cot,
    small_all,
    w_in_all,
    w_out_all,
    xpad,
    gpad,
    current,
    conv,
    xhat,
    rstd,
    normed,
    hidden,
    slope,
    branch,
    narrow,
    g_branch,
    g_pre,
    sums,
    stage_in,
    stage_out,
    stage_small,
    half_in,
    half_out,
    half_small,
    got_in,
    got_out,
    got_small,
    flat,
    flat_small,
    wide_cut,
    cut_in,
    cut_out,
    part_in,
    part_out,
    total_in,
    total_out,
    last_in,
    last_out,
    local_sem,
    small_send,
    small_recv,
    wi_send,
    wi_recv,
    wo_send,
    wo_recv,
    ci_send,
    ci_recv,
    co_send,
    co_recv,
    a_send,
    a_recv,
    b_send,
    b_recv,
    c_send,
    c_recv,
    d_send,
    d_recv,
):
    blocks, channels, units = w_in_all.shape
    rows, cols = image.shape[0], image.shape[1]
    positions = rows * cols
    chunks = channels // LANES
    tile = 2 * cols
    n_tiles = positions // tile
    each = channels // (NZ * NY * NC)
    span = each * NY
    wide_half = units // 2

    me = lax.axis_index("segment")
    dp = lax.axis_index("dp")
    core = lax.rem(dp, NC)
    y = lax.rem(dp // NC, NY)
    z = dp // (NC * NY)
    mate = dp + 1 - 2 * core

    def device(z_to, y_to):
        return (z_to * NY + y_to) * NC + core

    def shifted(base, by, size):
        return lax.rem(base + by, size)

    def remote(src, dst, ssem, rsem, to_dp, to_x):
        return pltpu.make_async_remote_copy(
            src_ref=src,
            dst_ref=dst,
            send_sem=ssem,
            recv_sem=rsem,
            device_id=(to_dp, to_x),
            device_id_type=MESH,
        )

    def arrived(ref, sem):
        pltpu.make_async_copy(ref, ref, sem).wait()

    image_copy = pltpu.make_async_copy(images_ref.at[me], image, local_sem.at[0])
    cot_copy = pltpu.make_async_copy(cot_ref.at[me], cot, local_sem.at[1])
    in_copy = pltpu.make_async_copy(w_in_ref.at[0], w_in_all.at[me], local_sem.at[2])
    out_copy = pltpu.make_async_copy(w_out_ref.at[0], w_out_all.at[me], local_sem.at[3])
    for copy in (image_copy, cot_copy, in_copy, out_copy):
        copy.start()
    barrier = pltpu.get_barrier_semaphore()
    pl.semaphore_signal(barrier, inc=1, device_id=(mate, me), device_id_type=MESH)
    for k in range(1, NX):
        pl.semaphore_signal(
            barrier, inc=1, device_id=(dp, shifted(me, k, NX)), device_id_type=MESH
        )
    for k in range(1, NZ):
        pl.semaphore_signal(
            barrier, inc=1, device_id=(device(shifted(z, k, NZ), y), me), device_id_type=MESH
        )
    for k in range(1, NY):
        pl.semaphore_signal(
            barrier, inc=1, device_id=(device(z, shifted(y, k, NY)), me), device_id_type=MESH
        )
    for t in range(49):
        small_all[me, t : t + 1, :] = kernels_ref[t]
    small_all[me, 49:50, :] = gains_ref[...]
    small_all[me, 50:51, :] = scales_ref[...]
    small_all[me, 51:56, :] = jnp.zeros((5, channels), F32)
    xpad[...] = jnp.zeros_like(xpad)
    gpad[...] = jnp.zeros_like(gpad)
    sums[...] = jnp.zeros_like(sums)
    wide_cut[...] = jnp.zeros_like(wide_cut)
    pl.semaphore_wait(barrier, 1 + (NX - 1) + (NZ - 1) + (NY - 1))

    right, left = shifted(me, 1, NX), shifted(me, NX - 1, NX)
    in_rows = pl.ds(pl.multiple_of(core * (channels // 2), 64), channels // 2)
    out_rows = pl.ds(pl.multiple_of(core * (units // 2), 64), units // 2)

    def small_push(k):
        return remote(
            small_all.at[me],
            small_all.at[me],
            small_send.at[k - 1],
            small_recv.at[NX - k - 1],
            dp,
            shifted(me, k, NX),
        )

    def in_push(slot, k, src, shard, to_x):
        return remote(
            src, w_in_all.at[shard, in_rows], wi_send.at[slot], wi_recv.at[k - 1], dp, to_x
        )

    def out_push(slot, k, src, shard, to_x):
        return remote(
            src, w_out_all.at[shard, out_rows], wo_send.at[slot], wo_recv.at[k - 1], dp, to_x
        )

    in_own, out_own = w_in_ref.at[0, in_rows], w_out_ref.at[0, out_rows]
    smalls = [small_push(k) for k in range(1, NX)]
    to_right = [in_push(0, 3, in_own, me, right), out_push(0, 3, out_own, me, right)]
    to_left = [out_push(1, 1, out_own, me, left), in_push(1, 1, in_own, me, left)]
    pushes = smalls + to_right + to_left

    def start(copies):
        for copy in copies:
            copy.start()

    start(smalls + [to_right[0], to_left[0], to_left[1], to_right[1]])
    in_relay = in_push(2, 2, w_in_all.at[left, in_rows], left, right)
    out_relay = out_push(2, 2, w_out_all.at[right, out_rows], right, left)

    def in_mate(shard, k):
        part = w_in_all.at[shard, in_rows]
        return remote(part, part, ci_send.at[k - 1], ci_recv.at[k - 1], mate, me)

    def out_mate(shard, k):
        part = w_out_all.at[shard, out_rows]
        return remote(part, part, co_send.at[k - 1], co_recv.at[k - 1], mate, me)

    def relay_in():
        arrived(w_in_all.at[left, in_rows], wi_recv.at[2])
        in_relay.start()

    def relay_out():
        arrived(w_out_all.at[right, out_rows], wo_recv.at[0])
        out_relay.start()

    def arrive(shard):
        for k in range(1, NX):

            @pl.when(lax.rem(shard - me + NX, NX) == k)
            def _():
                if k != 3:
                    arrived(w_in_all.at[shard, in_rows], wi_recv.at[k - 1])
                in_mate(shard, k).start()
                if k != 1:
                    arrived(w_out_all.at[shard, out_rows], wo_recv.at[k - 1])
                out_mate(shard, k).start()

    def complete(shard):
        @pl.when(shard == me)
        def _():
            in_copy.wait()
            out_copy.wait()

        for k in range(1, NX):

            @pl.when(lax.rem(shard - me + NX, NX) == k)
            def _():
                arrived(w_in_all.at[shard, in_rows], ci_recv.at[k - 1])
                arrived(w_out_all.at[shard, out_rows], co_recv.at[k - 1])

    def lanes(c):
        return slice(c * LANES, (c + 1) * LANES)

    ways = {0: (stage_in, half_in, got_in), 1: (stage_out, half_out, got_out)}
    ways[2] = (stage_small, half_small, got_small)
    cuts = {0: (cut_in, part_in, total_in, last_in), 1: (cut_out, part_out, total_out, last_out)}

    def a_copy(s, p):
        stage, half, _ = ways[p]
        return remote(
            stage.at[s, 1 - core], half.at[s], a_send.at[s, p], a_recv.at[s, p], mate, me
        )

    def b_copies(s, p):
        _, half, got = ways[p]
        found = []
        for k in range(1, NZ):
            at = shifted(y if p == 1 else z, k, NZ)
            to = device(z, at) if p == 1 else device(at, y)
            found.append(
                remote(
                    half.at[s, at], got.at[s, k - 1], b_send.at[s, p, 0], b_recv.at[s, p, 0], to, me
                )
            )
        return found

    def hops(s, p, step):
        _, half, got = ways[p]
        here = y if p == 1 else z
        found = []
        for slot, by, to in ((step - 1, 5 - step, 1), (step + 3, NZ - 4 + step, NZ - 1)):
            if slot == step + 3 and step == 4:
                continue
            at, to = shifted(here, by, NZ), shifted(here, to, NZ)
            to = device(z, to) if p == 1 else device(to, y)
            copy = remote(
                half.at[s, at], got.at[s, slot], b_send.at[s, p, slot], b_recv.at[s, p, slot], to, me
            )
            found.append((copy, slot, at))
        return found

    def hop(s, step):
        for p in (1, 0):
            _, half, got = ways[p]
            for copy, slot, at in hops(s, p, step):
                if step > 1:
                    arrived(got.at[s, slot - 1], b_recv.at[s, p, slot - 1])
                    value = half[s, at].astype(F32) + got[s, slot - 1].astype(F32)
                    half[s, at] = value.astype(BF16)
                copy.start()

    def c_copies(q, p):
        cut, part = cuts[p][:2]
        found = []
        for k in range(1, NZ):
            at = shifted(z if p == 1 else y, k, NZ)
            to = device(at, y) if p == 1 else device(z, at)
            found.append(
                remote(cut.at[q, at], part.at[q, k - 1], c_send.at[q, p], c_recv.at[q, p], to, me)
            )
        return found

    def d_copies(p):
        total, last = cuts[p][2:]
        found = []
        for k in range(1, NX):
            at = shifted(me, k, NX)
            found.append(
                remote(total.at[at], last.at[k - 1], d_send.at[p], d_recv.at[p], dp, at)
            )
        return found

    def pair_sum(s, p):
        stage, half, _ = ways[p]
        arrived(half.at[s], a_recv.at[s, p])

        def add(i, carry):
            value = half[s, i].astype(F32) + stage[s, core, i].astype(F32)
            half[s, i] = value.astype(half.dtype)
            return carry

        lax.fori_loop(0, NZ, add, 0, unroll=2)

    def spread(s, p):
        for copy in b_copies(s, p):
            copy.start()

    def line_sum(s, p, direct):
        _, half, got = ways[p]
        value = half[s, y if p == 1 else z].astype(F32)
        if direct:
            arrived(got.at[s], b_recv.at[s, p, 0])
            ends = range(NZ - 1)
        else:
            ends = (3, 6)
            for k in ends:
                arrived(got.at[s, k], b_recv.at[s, p, k])
        for k in ends:
            value = value + got[s, k].astype(F32)
        if p == 2:
            flat_small[...] = value
            for i in range(NY):
                for j in range(each):
                    row = flat_small[each * i + j : each * i + j + 1, :]
                    for b in range(2):
                        wide_cut[0, s, i, b, 2 * each : 2 * each + 1, lanes(j)] = row
            return
        flat[...] = value
        q, b = 1 - s // 2, lax.rem(s, 2)
        for i in range(NY):
            wide_cut[p, q, i, b, 0:each, :] = flat[each * i : each * i + each, :]
            wide_cut[p, q, i, b, each : 2 * each, :] = flat[span + each * i : span + each * i + each, :]

    def gather(q):
        for p in (1, 0):
            for i in range(NY):
                cuts[p][0][q, i] = wide_cut[p, q, i].reshape(16, wide_half).astype(BF16)
            for copy in c_copies(q, p):
                copy.start()

    def plane_sum(q):
        for p in (1, 0):
            cut, part, total, _ = cuts[p]
            arrived(part.at[q], c_recv.at[q, p])
            value = cut[q, z if p == 1 else y].astype(F32)
            for k in range(NY - 1):
                value = value + part[q, k].astype(F32)
            first = 2 * (1 - q)
            total[first : first + 2] = value.reshape(2, 8, wide_half)


    def taps(s, c, q):
        return [
            jnp.broadcast_to(
                small_all[s, pl.ds(7 * r + q, 1), pl.ds(pl.multiple_of(c * LANES, LANES), LANES)],
                (8, LANES),
            )
            for r in range(7)
        ]

    image_copy.wait()
    current[...] = image[...].reshape(positions, channels).astype(F32)
    def forward(s, carry):
        def store_row(i, carry):
            for c in range(chunks):
                xpad[s, c, i, PAD : PAD + cols, :] = current[
                    pl.ds(pl.multiple_of(i * cols, cols), cols), lanes(c)
                ]
            return carry

        lax.fori_loop(0, rows, store_row, 0, unroll=4)
        for k in range(1, NX):

            @pl.when(lax.rem(s - me + NX, NX) == k)
            def _():
                arrived(small_all.at[s], small_recv.at[k - 1])


        def conv_chunk(c, carry):
            acc = [[None, None] for _ in range(rows)]
            for q in range(7):
                weights = taps(s, c, q)
                for i in range(rows):
                    for half in range(cols // 8):
                        value = xpad[s, c, i, PAD - 3 + q + 8 * half : PAD + 5 + q + 8 * half, :]
                        for r in range(7):
                            o = i - r + 3
                            if 0 <= o < rows:
                                term = weights[r] * value
                                old = acc[o][half]
                                acc[o][half] = term if old is None else old + term
            for o in range(rows):
                for half in range(cols // 8):
                    conv[c, o * cols + 8 * half : o * cols + 8 * half + 8, :] = acc[o][half]
            return carry

        lax.fori_loop(0, chunks, conv_chunk, 0)

        gain = small_all[s, 49:50, :]
        scale = small_all[s, 50:51, :]

        def norm_tile(t, carry):
            at = pl.ds(pl.multiple_of(t * tile, tile), tile)
            parts = [conv[c, at, :] for c in range(chunks)]
            mean = jnp.sum(sum(parts), axis=1, keepdims=True) * (1.0 / channels)
            parts = [p - mean for p in parts]
            var = jnp.sum(sum(p * p for p in parts), axis=1, keepdims=True) * (1.0 / channels)
            inverse = lax.rsqrt(var + EPS)
            rstd[s, at, :] = jnp.broadcast_to(inverse, (tile, LANES))
            for c in range(chunks):
                value = parts[c] * inverse
                xhat[s, at, lanes(c)] = value
                normed[s, at, lanes(c)] = (value * gain[:, lanes(c)]).astype(BF16)
            return carry

        lax.fori_loop(0, n_tiles, norm_tile, 0, unroll=8)

        @pl.when(s == 0)
        def _():
            relay_in()
            relay_out()
            arrive(s)

        complete(s)
        for n in range(0, units, 256):
            some = slice(n, n + 256)
            tall = product(normed[s], w_in_all[s, :, some])
            for m in range(0, positions, 16):
                at = slice(m, m + 16)
                value = tall[at]
                square = value * value
                gate = jnp.tanh(GELU_A * value * (1.0 + GELU_B * square))
                half = 0.5 * (1.0 + gate)
                hidden[s, at, some] = (value * half).astype(BF16)
                slope[s, at, some] = half + (0.5 * GELU_A) * value * (1.0 - gate * gate) * (
                    1.0 + (3.0 * GELU_B) * square
                )
        branch[s] = product(hidden[s], w_out_all[s])

        @pl.when(s < blocks - 1)
        def _():
            arrive(s + 1)

        def residual_tile(t, carry):
            at = pl.ds(pl.multiple_of(t * tile, tile), tile)
            current[at, :] = current[at, :] + scale * branch[s, at, :]
            return carry

        lax.fori_loop(0, n_tiles, residual_tile, 0, unroll=2)
        return carry

    lax.fori_loop(0, blocks, forward, 0)
    cot_copy.wait()
    current[...] = cot[...].reshape(positions, channels).astype(F32)

    def backward(step, carry):
        s = blocks - 1 - step
        gain = small_all[s, 49:50, :]
        scale = small_all[s, 50:51, :]

        def scale_tile(t, total):
            at = pl.ds(pl.multiple_of(t * tile, tile), tile)
            value = current[at, :]
            g_branch[at, :] = (value * scale).astype(BF16)
            return total + jnp.sum((value * branch[s, at, :]).reshape(tile // 8, 8, channels), axis=0)

        total = lax.fori_loop(0, n_tiles, scale_tile, jnp.zeros((8, channels), F32), unroll=2)
        sums[lax.rem(s, 2), 50:51, :] = jnp.sum(total, axis=0, keepdims=True)
        def staged(stage, order, kept, other):
            turned = product_nt(order_ref[order], kept).astype(BF16)
            for h in range(NC):
                lo = h * (channels // 2)
                value = product(turned[lo : lo + channels // 2], other)
                for i in range(NZ):
                    piece = value[i * span : (i + 1) * span]
                    stage[s, h, i] = jnp.concatenate(
                        [piece[:, :wide_half], piece[:, wide_half:]], axis=0
                    ).astype(BF16)

        staged(stage_out, 1, g_branch[...], hidden[s])
        a_copy(s, 1).start()
        for n in range(0, units, 256):
            some = slice(n, n + 256)
            tall = product_nt(g_branch[...], w_out_all[s, some, :])
            for m in range(0, positions, 16):
                at = slice(m, m + 16)
                g_pre[at, some] = (tall[at] * slope[s, at, some]).astype(BF16)

        staged(stage_in, 0, normed[s], g_pre[...])
        a_copy(s, 0).start()
        narrow[...] = product_nt(g_pre[...], w_in_all[s])

        @pl.when(step >= 1)
        def _():
            hop(s + 1, 2)

        @pl.when(step >= 3)
        def _():
            line_sum(s + 3, 1, False)
            line_sum(s + 3, 0, False)
            line_sum(0, 2, True)


        def norm_row(i, total):
            at = pl.ds(pl.multiple_of(i * cols, cols), cols)
            grad = narrow[at, :]
            hat = xhat[s, at, :]
            both = grad * hat
            total = total + jnp.sum(both.reshape(cols // 8, 8, channels), axis=0)
            grad = grad * gain
            both = both * gain
            mean = jnp.sum(
                sum(grad[:, lanes(c)] for c in range(chunks)), axis=1, keepdims=True
            ) * (1.0 / channels)
            cross = jnp.sum(
                sum(both[:, lanes(c)] for c in range(chunks)), axis=1, keepdims=True
            ) * (1.0 / channels)
            inverse = rstd[s, at, :]
            for c in range(chunks):
                gpad[c, i, PAD : PAD + cols, :] = inverse * (
                    grad[:, lanes(c)] - mean - hat[:, lanes(c)] * cross
                )
            return total

        total = lax.fori_loop(0, rows, norm_row, jnp.zeros((8, channels), F32), unroll=16)
        slot = lax.rem(s, 2)
        sums[slot, 49:50, :] = jnp.sum(total, axis=0, keepdims=True)

        pair_sum(s, 1)
        pair_sum(s, 0)

        @pl.when(s > 0)
        def _():
            hop(s, 1)

        @pl.when(s == 0)
        def _():
            spread(0, 1)
            spread(0, 0)

        @pl.when(step >= 2)
        def _():
            hop(s + 2, 4)

        @pl.when(step == 2)
        def _():
            pair_sum(0, 2)
            spread(0, 2)


        def conv_chunk(c, carry):
            at_c = pl.ds(pl.multiple_of(c * LANES, LANES), LANES)
            acc = [[None, None] for _ in range(rows)]
            for q in range(7):
                weights = taps(s, c, q)
                for i in range(rows):
                    for half in range(cols // 8):
                        start = PAD + 3 - q + 8 * half
                        value = gpad[c, i, start : start + 8, :]
                        for r in range(7):
                            o = i + r - 3
                            if 0 <= o < rows:
                                term = weights[r] * value
                                old = acc[o][half]
                                acc[o][half] = term if old is None else old + term
            for o in range(rows):
                for half in range(cols // 8):
                    at = slice(o * cols + 8 * half, o * cols + 8 * half + 8)
                    current[at, at_c] = current[at, at_c] + acc[o][half]
            return carry

        @pl.when(s > 0)
        def _():
            lax.fori_loop(0, chunks, conv_chunk, 0)


        def kernel_chunk(c, carry):
            at_c = pl.ds(pl.multiple_of(c * LANES, LANES), LANES)
            grads = [
                [gpad[c, o, PAD + 8 * half : PAD + 8 * half + 8, :] for half in range(cols // 8)]
                for o in range(rows)
            ]
            for q in range(7):
                acc = [None] * 7
                for i in range(rows):
                    for half in range(cols // 8):
                        value = xpad[s, c, i, PAD - 3 + q + 8 * half : PAD + 5 + q + 8 * half, :]
                        for r in range(7):
                            o = i - r + 3
                            if 0 <= o < rows:
                                term = grads[o][half] * value
                                acc[r] = term if acc[r] is None else acc[r] + term
                for r in range(7):
                    sums[slot, 7 * r + q : 7 * r + q + 1, at_c] = jnp.sum(acc[r], axis=0, keepdims=True)
            return carry

        lax.fori_loop(0, chunks, kernel_chunk, 0)

        @pl.when(step >= 1)
        def _():
            hop(s + 1, 3)

        @pl.when(lax.rem(step, 2) == 1)
        def _():
            pair = step // 2
            value = product_nt(order_ref[0], sums[...].reshape(LANES, channels).astype(BF16))
            for h in range(NC):
                for i in range(NZ):
                    lo = h * (channels // 2) + i * span
                    stage_small[pair, h, i] = value[lo : lo + span]
            a_copy(pair, 2).start()

        return carry

    lax.fori_loop(0, blocks, backward, 0)
    hop(1, 4)
    for p in (1, 0):
        line_sum(2, p, False)
    gather(0)
    pair_sum(1, 2)
    spread(1, 2)
    for p in (1, 0):
        line_sum(1, p, False)
    for p in (1, 0):
        line_sum(0, p, True)
    line_sum(1, 2, True)
    gather(1)
    plane_sum(0)
    plane_sum(1)
    last = d_copies(1) + d_copies(0)
    for copy in last:
        copy.start()
    for p in (1, 0):
        total, tail = cuts[p][2:]
        arrived(tail, d_recv.at[p])
        value = total[me]
        for k in range(NX - 1):
            value = value + tail[k]
        ref = grad_out_ref if p == 1 else grad_in_ref
        for j in range(each):
            ref[j, :, :wide_half] = value[j : j + 1, :]
            ref[j, :, wide_half:] = value[each + j : each + j + 1, :]
        if p == 0:
            lane = lax.broadcasted_iota(jnp.int32, (1, LANES), 1)
            gain = scale = jnp.zeros((1, LANES), F32)
            for j in range(each):
                row = value[2 * each : 2 * each + 1, lanes(j)]
                row = jnp.where(lax.rem(me, 2) == 1, row[:, LANES // 2 :], row[:, : LANES // 2])
                grad_kernel_ref[j] = row[:, :49]
                gain = jnp.where(lane == j, jnp.broadcast_to(row[:, 49:50], (1, LANES)), gain)
                scale = jnp.where(lane == j, jnp.broadcast_to(row[:, 50:51], (1, LANES)), scale)
            grad_gain_ref[...] = gain[:, :each]
            grad_scale_ref[...] = scale[:, :each]

    for copy in pushes + [in_relay, out_relay] + last:
        copy.wait_send()
    for k in range(1, NX):
        shard = shifted(me, k, NX)
        in_mate(shard, k).wait_send()
        out_mate(shard, k).wait_send()

    def left_here(ref, sem):
        pltpu.make_async_copy(ref, ref, sem).wait()

    def drain(s, carry):
        for p in (0, 1):
            left_here(ways[p][1].at[s], a_send.at[s, p])

            @pl.when(s > 0)
            def _():
                for k in range(NZ - 1):
                    left_here(ways[p][2].at[s, k], b_send.at[s, p, k])

        return carry

    lax.fori_loop(0, blocks, drain, 0)
    for p in (0, 1):
        left_here(ways[p][2].at[0], b_send.at[0, p, 0])
    for q in range(2):
        left_here(half_small.at[q], a_send.at[q, 2])
        left_here(got_small.at[q], b_send.at[q, 2, 0])
        for p in (0, 1):
            left_here(cuts[p][1].at[q], c_send.at[q, p])


def local(images, cotangent, kernels, norm_gains, w_in, w_out, scales):
    channels, units = w_in.shape[1:]
    rows, cols = images.shape[1:3]
    positions = rows * cols
    blocks = NX
    chunks = channels // LANES
    each = channels // (NZ * NY * NC)
    span = each * NY
    wide_half = units // 2
    orders = jnp.asarray(send_orders(channels), BF16)
    vmem = pl.BlockSpec(memory_space=pltpu.VMEM)
    anywhere = pl.BlockSpec(memory_space=pl.ANY)
    dma = pltpu.SemaphoreType.DMA
    grad_in, grad_out, grad_kernel, grad_gain, grad_scale = pl.pallas_call(
        block_kernel,
        out_shape=[
            jax.ShapeDtypeStruct((each, 1, units), F32),
            jax.ShapeDtypeStruct((each, 1, units), F32),
            jax.ShapeDtypeStruct((each, 1, 49), F32),
            jax.ShapeDtypeStruct((1, each), F32),
            jax.ShapeDtypeStruct((1, each), F32),
        ],
        in_specs=[anywhere, anywhere, vmem, vmem, vmem, anywhere, anywhere, vmem],
        out_specs=[vmem] * 5,
        scratch_shapes=[
            pltpu.VMEM((rows, cols, channels), BF16),
            pltpu.VMEM((rows, cols, channels), BF16),
            pltpu.VMEM((blocks, 56, channels), F32),
            pltpu.VMEM((blocks, channels, units), BF16),
            pltpu.VMEM((blocks, units, channels), BF16),
            pltpu.VMEM((blocks, chunks, rows, cols + 2 * PAD, LANES), F32),
            pltpu.VMEM((chunks, rows, cols + 2 * PAD, LANES), F32),
            pltpu.VMEM((positions, channels), F32),
            pltpu.VMEM((chunks, positions, LANES), F32),
            pltpu.VMEM((blocks, positions, channels), F32),
            pltpu.VMEM((blocks, positions, LANES), F32),
            pltpu.VMEM((blocks, positions, channels), BF16),
            pltpu.VMEM((blocks, positions, units), BF16),
            pltpu.VMEM((blocks, positions, units), F32),
            pltpu.VMEM((blocks, positions, channels), F32),
            pltpu.VMEM((positions, channels), F32),
            pltpu.VMEM((positions, channels), BF16),
            pltpu.VMEM((positions, units), BF16),
            pltpu.VMEM((2, LANES // 2, channels), F32),
            pltpu.VMEM((blocks, NC, NZ, 2 * span, wide_half), BF16),
            pltpu.VMEM((blocks, NC, NZ, 2 * span, wide_half), BF16),
            pltpu.VMEM((blocks // 2, NC, NZ, span, LANES), F32),
            pltpu.VMEM((blocks, NZ, 2 * span, wide_half), BF16),
            pltpu.VMEM((blocks, NZ, 2 * span, wide_half), BF16),
            pltpu.VMEM((blocks // 2, NZ, span, LANES), F32),
            pltpu.VMEM((blocks, NZ - 1, 2 * span, wide_half), BF16),
            pltpu.VMEM((blocks, NZ - 1, 2 * span, wide_half), BF16),
            pltpu.VMEM((blocks // 2, NZ - 1, span, LANES), F32),
            pltpu.VMEM((2 * span, wide_half), F32),
            pltpu.VMEM((span, LANES), F32),
            pltpu.VMEM((2, blocks // 2, NY, 2, 8, wide_half), F32),
            pltpu.VMEM((blocks // 2, NY, 16, wide_half), BF16),
            pltpu.VMEM((blocks // 2, NY, 16, wide_half), BF16),
            pltpu.VMEM((blocks // 2, NY - 1, 16, wide_half), BF16),
            pltpu.VMEM((blocks // 2, NY - 1, 16, wide_half), BF16),
            pltpu.VMEM((blocks, 8, wide_half), F32),
            pltpu.VMEM((blocks, 8, wide_half), F32),
            pltpu.VMEM((NX - 1, 8, wide_half), F32),
            pltpu.VMEM((NX - 1, 8, wide_half), F32),
            dma((4,)),
            dma((NX - 1,)),
            dma((NX - 1,)),
            dma((3,)),
            dma((NX - 1,)),
            dma((3,)),
            dma((NX - 1,)),
            dma((NX - 1,)),
            dma((NX - 1,)),
            dma((NX - 1,)),
            dma((NX - 1,)),
            dma((blocks, 3)),
            dma((blocks, 3)),
            dma((blocks, 3, NZ - 1)),
            dma((blocks, 3, NZ - 1)),
            dma((blocks, 3)),
            dma((blocks, 3)),
            dma((3,)),
            dma((3,)),
        ],
        compiler_params=pltpu.CompilerParams(
            vmem_limit_bytes=60 * 1024 * 1024, collective_id=0, has_side_effects=True
        ),
        name="blocks",
    )(images, cotangent, kernels.transpose(1, 0, 2), norm_gains, scales, w_in, w_out, orders)
    return (
        grad_kernel.transpose(1, 2, 0),
        grad_gain,
        grad_in.transpose(1, 0, 2),
        grad_out.transpose(1, 2, 0),
        grad_scale,
    )


def solution(mesh):
    in_specs = (
        P("dp", None, None, None),
        P("dp", None, None, None),
        P("segment", None, None),
        P("segment", None),
        P("segment", None, None),
        P("segment", None, None),
        P("segment", None),
    )
    out_specs = (
        P("segment", None, "dp"),
        P("segment", "dp"),
        P("segment", "dp", None),
        P("segment", None, "dp"),
        P("segment", "dp"),
    )
    return jax.shard_map(local, mesh=mesh, in_specs=in_specs, out_specs=out_specs, check_vma=False)
```

```python
import math

import jax
import jax.numpy as jnp
import numpy as np
from jax import lax
from jax.experimental import pallas as pl
from jax.experimental.pallas import tpu as pltpu
from jax.sharding import PartitionSpec as P

EPS = 1e-06
LANES = 128
PAD = 8
GELU_A = math.sqrt(2.0 / math.pi)
GELU_B = 0.044715
F32 = jnp.float32
BF16 = jnp.bfloat16
NX, NY, NZ, NC = 4, 8, 8, 2
MESH = pl.DeviceIdType.MESH


def product(a, b):
    return jnp.dot(a, b, preferred_element_type=F32)


def product_nt(a, b):
    return lax.dot_general(a, b, (((1,), (1,)), ((), ())), preferred_element_type=F32)


def send_orders(channels):
    each = channels // (NZ * NY * NC)
    number = np.arange(channels).reshape(NZ, NY, NC, each)
    rows = [number.transpose(2, 0, 1, 3).reshape(-1), number.transpose(2, 1, 0, 3).reshape(-1)]
    return np.stack([np.eye(channels, dtype=np.float32)[r] for r in rows])


def block_kernel(
    images_ref,
    cot_ref,
    kernels_ref,
    gains_ref,
    scales_ref,
    w_in_ref,
    w_out_ref,
    order_ref,
    grad_in_ref,
    grad_out_ref,
    grad_kernel_ref,
    grad_gain_ref,
    grad_scale_ref,
    image,
    cot,
    small_all,
    w_in_all,
    w_out_all,
    xpad,
    gpad,
    current,
    conv,
    xhat,
    rstd,
    normed,
    hidden,
    slope,
    branch,
    narrow,
    g_branch,
    g_pre,
    sums,
    stage_in,
    stage_out,
    stage_small,
    half_in,
    half_out,
    half_small,
    got_in,
    got_out,
    got_small,
    flat,
    flat_small,
    wide_cut,
    cut_in,
    cut_out,
    part_in,
    part_out,
    total_in,
    total_out,
    last_in,
    last_out,
    local_sem,
    small_send,
    small_recv,
    wi_send,
    wi_recv,
    wo_send,
    wo_recv,
    ci_send,
    ci_recv,
    co_send,
    co_recv,
    a_send,
    a_recv,
    b_send,
    b_recv,
    c_send,
    c_recv,
    d_send,
    d_recv,
):
    blocks, channels, units = w_in_all.shape
    rows, cols = image.shape[0], image.shape[1]
    positions = rows * cols
    chunks = channels // LANES
    tile = 2 * cols
    n_tiles = positions // tile
    each = channels // (NZ * NY * NC)
    span = each * NY
    wide_half = units // 2

    me = lax.axis_index("segment")
    dp = lax.axis_index("dp")
    core = lax.rem(dp, NC)
    y = lax.rem(dp // NC, NY)
    z = dp // (NC * NY)
    mate = dp + 1 - 2 * core

    def device(z_to, y_to):
        return (z_to * NY + y_to) * NC + core

    def shifted(base, by, size):
        return lax.rem(base + by, size)

    def remote(src, dst, ssem, rsem, to_dp, to_x):
        return pltpu.make_async_remote_copy(
            src_ref=src,
            dst_ref=dst,
            send_sem=ssem,
            recv_sem=rsem,
            device_id=(to_dp, to_x),
            device_id_type=MESH,
        )

    def arrived(ref, sem):
        pltpu.make_async_copy(ref, ref, sem).wait()

    image_copy = pltpu.make_async_copy(images_ref.at[me], image, local_sem.at[0])
    cot_copy = pltpu.make_async_copy(cot_ref.at[me], cot, local_sem.at[1])
    in_copy = pltpu.make_async_copy(w_in_ref.at[0], w_in_all.at[me], local_sem.at[2])
    out_copy = pltpu.make_async_copy(w_out_ref.at[0], w_out_all.at[me], local_sem.at[3])
    for copy in (image_copy, cot_copy, in_copy, out_copy):
        copy.start()
    barrier = pltpu.get_barrier_semaphore()
    pl.semaphore_signal(barrier, inc=1, device_id=(mate, me), device_id_type=MESH)
    for k in range(1, NX):
        pl.semaphore_signal(
            barrier, inc=1, device_id=(dp, shifted(me, k, NX)), device_id_type=MESH
        )
    for k in range(1, NZ):
        pl.semaphore_signal(
            barrier, inc=1, device_id=(device(shifted(z, k, NZ), y), me), device_id_type=MESH
        )
    for k in range(1, NY):
        pl.semaphore_signal(
            barrier, inc=1, device_id=(device(z, shifted(y, k, NY)), me), device_id_type=MESH
        )
    for t in range(49):
        small_all[me, t : t + 1, :] = kernels_ref[t]
    small_all[me, 49:50, :] = gains_ref[...]
    small_all[me, 50:51, :] = scales_ref[...]
    small_all[me, 51:56, :] = jnp.zeros((5, channels), F32)
    xpad[...] = jnp.zeros_like(xpad)
    gpad[...] = jnp.zeros_like(gpad)
    sums[...] = jnp.zeros_like(sums)
    wide_cut[...] = jnp.zeros_like(wide_cut)
    pl.semaphore_wait(barrier, 1 + (NX - 1) + (NZ - 1) + (NY - 1))

    right, left = shifted(me, 1, NX), shifted(me, NX - 1, NX)
    in_rows = pl.ds(pl.multiple_of(core * (channels // 2), 64), channels // 2)
    out_rows = pl.ds(pl.multiple_of(core * (units // 2), 64), units // 2)

    def small_push(k):
        return remote(
            small_all.at[me],
            small_all.at[me],
            small_send.at[k - 1],
            small_recv.at[NX - k - 1],
            dp,
            shifted(me, k, NX),
        )

    def in_push(slot, k, src, shard, to_x):
        return remote(
            src, w_in_all.at[shard, in_rows], wi_send.at[slot], wi_recv.at[k - 1], dp, to_x
        )

    def out_push(slot, k, src, shard, to_x):
        return remote(
            src, w_out_all.at[shard, out_rows], wo_send.at[slot], wo_recv.at[k - 1], dp, to_x
        )

    in_own, out_own = w_in_ref.at[0, in_rows], w_out_ref.at[0, out_rows]
    smalls = [small_push(k) for k in range(1, NX)]
    to_right = [in_push(0, 3, in_own, me, right), out_push(0, 3, out_own, me, right)]
    to_left = [out_push(1, 1, out_own, me, left), in_push(1, 1, in_own, me, left)]
    pushes = smalls + to_right + to_left

    def start(copies):
        for copy in copies:
            copy.start()

    start(smalls + [to_right[0], to_left[0], to_left[1], to_right[1]])
    in_relay = in_push(2, 2, w_in_all.at[left, in_rows], left, right)
    out_relay = out_push(2, 2, w_out_all.at[right, out_rows], right, left)

    def in_mate(shard, k):
        part = w_in_all.at[shard, in_rows]
        return remote(part, part, ci_send.at[k - 1], ci_recv.at[k - 1], mate, me)

    def out_mate(shard, k):
        part = w_out_all.at[shard, out_rows]
        return remote(part, part, co_send.at[k - 1], co_recv.at[k - 1], mate, me)

    def relay_in():
        arrived(w_in_all.at[left, in_rows], wi_recv.at[2])
        in_relay.start()

    def relay_out():
        arrived(w_out_all.at[right, out_rows], wo_recv.at[0])
        out_relay.start()

    def arrive(shard):
        for k in range(1, NX):

            @pl.when(lax.rem(shard - me + NX, NX) == k)
            def _():
                if k != 3:
                    arrived(w_in_all.at[shard, in_rows], wi_recv.at[k - 1])
                in_mate(shard, k).start()
                if k != 1:
                    arrived(w_out_all.at[shard, out_rows], wo_recv.at[k - 1])
                out_mate(shard, k).start()

    def complete(shard):
        @pl.when(shard == me)
        def _():
            in_copy.wait()
            out_copy.wait()

        for k in range(1, NX):

            @pl.when(lax.rem(shard - me + NX, NX) == k)
            def _():
                arrived(w_in_all.at[shard, in_rows], ci_recv.at[k - 1])
                arrived(w_out_all.at[shard, out_rows], co_recv.at[k - 1])

    def lanes(c):
        return slice(c * LANES, (c + 1) * LANES)

    ways = {0: (stage_in, half_in, got_in), 1: (stage_out, half_out, got_out)}
    ways[2] = (stage_small, half_small, got_small)
    cuts = {0: (cut_in, part_in, total_in, last_in), 1: (cut_out, part_out, total_out, last_out)}

    def a_copy(s, p):
        stage, half, _ = ways[p]
        return remote(
            stage.at[s, 1 - core], half.at[s], a_send.at[s, p], a_recv.at[s, p], mate, me
        )

    def b_copies(s, p):
        _, half, got = ways[p]
        found = []
        for k in range(1, NZ):
            at = shifted(y if p == 1 else z, k, NZ)
            to = device(z, at) if p == 1 else device(at, y)
            found.append(
                remote(
                    half.at[s, at], got.at[s, k - 1], b_send.at[s, p, 0], b_recv.at[s, p, 0], to, me
                )
            )
        return found

    def hops(s, p, step):
        _, half, got = ways[p]
        here = y if p == 1 else z
        found = []
        for slot, by, to in ((step - 1, 5 - step, 1), (step + 3, NZ - 4 + step, NZ - 1)):
            if slot == step + 3 and step == 4:
                continue
            at, to = shifted(here, by, NZ), shifted(here, to, NZ)
            to = device(z, to) if p == 1 else device(to, y)
            copy = remote(
                half.at[s, at], got.at[s, slot], b_send.at[s, p, slot], b_recv.at[s, p, slot], to, me
            )
            found.append((copy, slot, at))
        return found

    def hop(s, step):
        for p in (1, 0):
            _, half, got = ways[p]
            for copy, slot, at in hops(s, p, step):
                if step > 1:
                    arrived(got.at[s, slot - 1], b_recv.at[s, p, slot - 1])
                    value = half[s, at].astype(F32) + got[s, slot - 1].astype(F32)
                    half[s, at] = value.astype(BF16)
                copy.start()

    def c_copies(q, p):
        cut, part = cuts[p][:2]
        found = []
        for k in range(1, NZ):
            at = shifted(z if p == 1 else y, k, NZ)
            to = device(at, y) if p == 1 else device(z, at)
            found.append(
                remote(cut.at[q, at], part.at[q, k - 1], c_send.at[q, p], c_recv.at[q, p], to, me)
            )
        return found

    def d_copies(p):
        total, last = cuts[p][2:]
        found = []
        for k in range(1, NX):
            at = shifted(me, k, NX)
            found.append(
                remote(total.at[at], last.at[k - 1], d_send.at[p], d_recv.at[p], dp, at)
            )
        return found

    def pair_sum(s, p):
        stage, half, _ = ways[p]
        arrived(half.at[s], a_recv.at[s, p])

        def add(i, carry):
            value = half[s, i].astype(F32) + stage[s, core, i].astype(F32)
            half[s, i] = value.astype(half.dtype)
            return carry

        lax.fori_loop(0, NZ, add, 0, unroll=2)

    def spread(s, p):
        for copy in b_copies(s, p):
            copy.start()

    def line_sum(s, p, direct):
        _, half, got = ways[p]
        value = half[s, y if p == 1 else z].astype(F32)
        if direct:
            arrived(got.at[s], b_recv.at[s, p, 0])
            ends = range(NZ - 1)
        else:
            ends = (3, 6)
            for k in ends:
                arrived(got.at[s, k], b_recv.at[s, p, k])
        for k in ends:
            value = value + got[s, k].astype(F32)
        if p == 2:
            flat_small[...] = value
            for i in range(NY):
                for j in range(each):
                    row = flat_small[each * i + j : each * i + j + 1, :]
                    for b in range(2):
                        wide_cut[0, s, i, b, 2 * each : 2 * each + 1, lanes(j)] = row
            return
        flat[...] = value
        q, b = 1 - s // 2, lax.rem(s, 2)
        for i in range(NY):
            wide_cut[p, q, i, b, 0:each, :] = flat[each * i : each * i + each, :]
            wide_cut[p, q, i, b, each : 2 * each, :] = flat[span + each * i : span + each * i + each, :]

    def gather(q):
        for p in (1, 0):
            for i in range(NY):
                cuts[p][0][q, i] = wide_cut[p, q, i].reshape(16, wide_half).astype(BF16)
            for copy in c_copies(q, p):
                copy.start()

    def plane_sum(q):
        for p in (1, 0):
            cut, part, total, _ = cuts[p]
            arrived(part.at[q], c_recv.at[q, p])
            value = cut[q, z if p == 1 else y].astype(F32)
            for k in range(NY - 1):
                value = value + part[q, k].astype(F32)
            first = 2 * (1 - q)
            total[first : first + 2] = value.reshape(2, 8, wide_half)


    def taps(s, c, q):
        return [
            jnp.broadcast_to(
                small_all[s, pl.ds(7 * r + q, 1), pl.ds(pl.multiple_of(c * LANES, LANES), LANES)],
                (8, LANES),
            )
            for r in range(7)
        ]

    image_copy.wait()
    current[...] = image[...].reshape(positions, channels).astype(F32)
    def forward(s, carry):
        def store_row(i, carry):
            for c in range(chunks):
                xpad[s, c, i, PAD : PAD + cols, :] = current[
                    pl.ds(pl.multiple_of(i * cols, cols), cols), lanes(c)
                ]
            return carry

        lax.fori_loop(0, rows, store_row, 0, unroll=4)
        for k in range(1, NX):

            @pl.when(lax.rem(s - me + NX, NX) == k)
            def _():
                arrived(small_all.at[s], small_recv.at[k - 1])


        def conv_chunk(c, carry):
            acc = [[None, None] for _ in range(rows)]
            for q in range(7):
                weights = taps(s, c, q)
                for i in range(rows):
                    for half in range(cols // 8):
                        value = xpad[s, c, i, PAD - 3 + q + 8 * half : PAD + 5 + q + 8 * half, :]
                        for r in range(7):
                            o = i - r + 3
                            if 0 <= o < rows:
                                term = weights[r] * value
                                old = acc[o][half]
                                acc[o][half] = term if old is None else old + term
            for o in range(rows):
                for half in range(cols // 8):
                    conv[c, o * cols + 8 * half : o * cols + 8 * half + 8, :] = acc[o][half]
            return carry

        lax.fori_loop(0, chunks, conv_chunk, 0)

        gain = small_all[s, 49:50, :]
        scale = small_all[s, 50:51, :]

        def norm_tile(t, carry):
            at = pl.ds(pl.multiple_of(t * tile, tile), tile)
            parts = [conv[c, at, :] for c in range(chunks)]
            mean = jnp.sum(sum(parts), axis=1, keepdims=True) * (1.0 / channels)
            parts = [p - mean for p in parts]
            var = jnp.sum(sum(p * p for p in parts), axis=1, keepdims=True) * (1.0 / channels)
            inverse = lax.rsqrt(var + EPS)
            rstd[s, at, :] = jnp.broadcast_to(inverse, (tile, LANES))
            for c in range(chunks):
                value = parts[c] * inverse
                xhat[s, at, lanes(c)] = value
                normed[s, at, lanes(c)] = (value * gain[:, lanes(c)]).astype(BF16)
            return carry

        lax.fori_loop(0, n_tiles, norm_tile, 0, unroll=8)

        @pl.when(s == 0)
        def _():
            @pl.when(me != 0)
            def _():
                relay_in()
                relay_out()

            arrive(s)

        complete(s)
        for n in range(0, units, 256):
            some = slice(n, n + 256)
            tall = product(normed[s], w_in_all[s, :, some])
            for m in range(0, positions, 16):
                at = slice(m, m + 16)
                value = tall[at]
                square = value * value
                gate = jnp.tanh(GELU_A * value * (1.0 + GELU_B * square))
                half = 0.5 * (1.0 + gate)
                hidden[s, at, some] = (value * half).astype(BF16)
                slope[s, at, some] = half + (0.5 * GELU_A) * value * (1.0 - gate * gate) * (
                    1.0 + (3.0 * GELU_B) * square
                )
        branch[s] = product(hidden[s], w_out_all[s])

        @pl.when(jnp.logical_and(s == 0, me == 0))
        def _():
            relay_in()
            relay_out()

        @pl.when(s < blocks - 1)
        def _():
            arrive(s + 1)

        def residual_tile(t, carry):
            at = pl.ds(pl.multiple_of(t * tile, tile), tile)
            current[at, :] = current[at, :] + scale * branch[s, at, :]
            return carry

        lax.fori_loop(0, n_tiles, residual_tile, 0, unroll=2)
        return carry

    lax.fori_loop(0, blocks, forward, 0)
    cot_copy.wait()
    current[...] = cot[...].reshape(positions, channels).astype(F32)

    def backward(step, carry):
        s = blocks - 1 - step
        gain = small_all[s, 49:50, :]
        scale = small_all[s, 50:51, :]

        def scale_tile(t, total):
            at = pl.ds(pl.multiple_of(t * tile, tile), tile)
            value = current[at, :]
            g_branch[at, :] = (value * scale).astype(BF16)
            return total + jnp.sum((value * branch[s, at, :]).reshape(tile // 8, 8, channels), axis=0)

        total = lax.fori_loop(0, n_tiles, scale_tile, jnp.zeros((8, channels), F32), unroll=2)
        sums[lax.rem(s, 2), 50:51, :] = jnp.sum(total, axis=0, keepdims=True)
        def staged(stage, order, kept, other):
            turned = product_nt(order_ref[order], kept).astype(BF16)
            for h in range(NC):
                lo = h * (channels // 2)
                value = product(turned[lo : lo + channels // 2], other)
                for i in range(NZ):
                    piece = value[i * span : (i + 1) * span]
                    stage[s, h, i] = jnp.concatenate(
                        [piece[:, :wide_half], piece[:, wide_half:]], axis=0
                    ).astype(BF16)

        staged(stage_out, 1, g_branch[...], hidden[s])
        a_copy(s, 1).start()
        for n in range(0, units, 256):
            some = slice(n, n + 256)
            tall = product_nt(g_branch[...], w_out_all[s, some, :])
            for m in range(0, positions, 16):
                at = slice(m, m + 16)
                g_pre[at, some] = (tall[at] * slope[s, at, some]).astype(BF16)

        staged(stage_in, 0, normed[s], g_pre[...])
        a_copy(s, 0).start()
        narrow[...] = product_nt(g_pre[...], w_in_all[s])

        @pl.when(step >= 1)
        def _():
            hop(s + 1, 2)

        @pl.when(step >= 3)
        def _():
            line_sum(s + 3, 1, False)
            line_sum(s + 3, 0, False)
            line_sum(0, 2, True)


        def norm_row(i, total):
            at = pl.ds(pl.multiple_of(i * cols, cols), cols)
            grad = narrow[at, :]
            hat = xhat[s, at, :]
            both = grad * hat
            total = total + jnp.sum(both.reshape(cols // 8, 8, channels), axis=0)
            grad = grad * gain
            both = both * gain
            mean = jnp.sum(
                sum(grad[:, lanes(c)] for c in range(chunks)), axis=1, keepdims=True
            ) * (1.0 / channels)
            cross = jnp.sum(
                sum(both[:, lanes(c)] for c in range(chunks)), axis=1, keepdims=True
            ) * (1.0 / channels)
            inverse = rstd[s, at, :]
            for c in range(chunks):
                gpad[c, i, PAD : PAD + cols, :] = inverse * (
                    grad[:, lanes(c)] - mean - hat[:, lanes(c)] * cross
                )
            return total

        total = lax.fori_loop(0, rows, norm_row, jnp.zeros((8, channels), F32), unroll=16)
        slot = lax.rem(s, 2)
        sums[slot, 49:50, :] = jnp.sum(total, axis=0, keepdims=True)

        pair_sum(s, 1)
        pair_sum(s, 0)

        @pl.when(s > 0)
        def _():
            hop(s, 1)

        @pl.when(s == 0)
        def _():
            spread(0, 1)
            spread(0, 0)

        @pl.when(step >= 2)
        def _():
            hop(s + 2, 4)

        @pl.when(step == 2)
        def _():
            pair_sum(0, 2)
            spread(0, 2)


        def conv_chunk(c, carry):
            at_c = pl.ds(pl.multiple_of(c * LANES, LANES), LANES)
            acc = [[None, None] for _ in range(rows)]
            for q in range(7):
                weights = taps(s, c, q)
                for i in range(rows):
                    for half in range(cols // 8):
                        start = PAD + 3 - q + 8 * half
                        value = gpad[c, i, start : start + 8, :]
                        for r in range(7):
                            o = i + r - 3
                            if 0 <= o < rows:
                                term = weights[r] * value
                                old = acc[o][half]
                                acc[o][half] = term if old is None else old + term
            for o in range(rows):
                for half in range(cols // 8):
                    at = slice(o * cols + 8 * half, o * cols + 8 * half + 8)
                    current[at, at_c] = current[at, at_c] + acc[o][half]
            return carry

        @pl.when(s > 0)
        def _():
            lax.fori_loop(0, chunks, conv_chunk, 0)


        def kernel_chunk(c, carry):
            at_c = pl.ds(pl.multiple_of(c * LANES, LANES), LANES)
            grads = [
                [gpad[c, o, PAD + 8 * half : PAD + 8 * half + 8, :] for half in range(cols // 8)]
                for o in range(rows)
            ]
            for q in range(7):
                acc = [None] * 7
                for i in range(rows):
                    for half in range(cols // 8):
                        value = xpad[s, c, i, PAD - 3 + q + 8 * half : PAD + 5 + q + 8 * half, :]
                        for r in range(7):
                            o = i - r + 3
                            if 0 <= o < rows:
                                term = grads[o][half] * value
                                acc[r] = term if acc[r] is None else acc[r] + term
                for r in range(7):
                    sums[slot, 7 * r + q : 7 * r + q + 1, at_c] = jnp.sum(acc[r], axis=0, keepdims=True)
            return carry

        lax.fori_loop(0, chunks, kernel_chunk, 0)

        @pl.when(step >= 1)
        def _():
            hop(s + 1, 3)

        @pl.when(lax.rem(step, 2) == 1)
        def _():
            pair = step // 2
            value = product_nt(order_ref[0], sums[...].reshape(LANES, channels).astype(BF16))
            for h in range(NC):
                for i in range(NZ):
                    lo = h * (channels // 2) + i * span
                    stage_small[pair, h, i] = value[lo : lo + span]
            a_copy(pair, 2).start()

        return carry

    lax.fori_loop(0, blocks, backward, 0)
    pair_sum(1, 2)
    spread(1, 2)
    hop(1, 4)
    for p in (1, 0):
        line_sum(2, p, False)
    gather(0)
    for p in (1, 0):
        line_sum(1, p, False)
    for p in (1, 0):
        line_sum(0, p, True)
    line_sum(1, 2, True)
    gather(1)
    plane_sum(0)
    plane_sum(1)
    last = d_copies(1) + d_copies(0)
    for copy in last:
        copy.start()
    for p in (1, 0):
        total, tail = cuts[p][2:]
        arrived(tail, d_recv.at[p])
        value = total[me]
        for k in range(NX - 1):
            value = value + tail[k]
        ref = grad_out_ref if p == 1 else grad_in_ref
        for j in range(each):
            ref[j, :, :wide_half] = value[j : j + 1, :]
            ref[j, :, wide_half:] = value[each + j : each + j + 1, :]
        if p == 0:
            lane = lax.broadcasted_iota(jnp.int32, (1, LANES), 1)
            gain = scale = jnp.zeros((1, LANES), F32)
            for j in range(each):
                row = value[2 * each : 2 * each + 1, lanes(j)]
                row = jnp.where(lax.rem(me, 2) == 1, row[:, LANES // 2 :], row[:, : LANES // 2])
                grad_kernel_ref[j] = row[:, :49]
                gain = jnp.where(lane == j, jnp.broadcast_to(row[:, 49:50], (1, LANES)), gain)
                scale = jnp.where(lane == j, jnp.broadcast_to(row[:, 50:51], (1, LANES)), scale)
            grad_gain_ref[...] = gain[:, :each]
            grad_scale_ref[...] = scale[:, :each]

    for copy in pushes + [in_relay, out_relay] + last:
        copy.wait_send()
    for k in range(1, NX):
        shard = shifted(me, k, NX)
        in_mate(shard, k).wait_send()
        out_mate(shard, k).wait_send()

    def left_here(ref, sem):
        pltpu.make_async_copy(ref, ref, sem).wait()

    def drain(s, carry):
        for p in (0, 1):
            left_here(ways[p][1].at[s], a_send.at[s, p])

            @pl.when(s > 0)
            def _():
                for k in range(NZ - 1):
                    left_here(ways[p][2].at[s, k], b_send.at[s, p, k])

        return carry

    lax.fori_loop(0, blocks, drain, 0)
    for p in (0, 1):
        left_here(ways[p][2].at[0], b_send.at[0, p, 0])
    for q in range(2):
        left_here(half_small.at[q], a_send.at[q, 2])
        left_here(got_small.at[q], b_send.at[q, 2, 0])
        for p in (0, 1):
            left_here(cuts[p][1].at[q], c_send.at[q, p])


def local(images, cotangent, kernels, norm_gains, w_in, w_out, scales):
    channels, units = w_in.shape[1:]
    rows, cols = images.shape[1:3]
    positions = rows * cols
    blocks = NX
    chunks = channels // LANES
    each = channels // (NZ * NY * NC)
    span = each * NY
    wide_half = units // 2
    orders = jnp.asarray(send_orders(channels), BF16)
    vmem = pl.BlockSpec(memory_space=pltpu.VMEM)
    anywhere = pl.BlockSpec(memory_space=pl.ANY)
    dma = pltpu.SemaphoreType.DMA
    grad_in, grad_out, grad_kernel, grad_gain, grad_scale = pl.pallas_call(
        block_kernel,
        out_shape=[
            jax.ShapeDtypeStruct((each, 1, units), F32),
            jax.ShapeDtypeStruct((each, 1, units), F32),
            jax.ShapeDtypeStruct((each, 1, 49), F32),
            jax.ShapeDtypeStruct((1, each), F32),
            jax.ShapeDtypeStruct((1, each), F32),
        ],
        in_specs=[anywhere, anywhere, vmem, vmem, vmem, anywhere, anywhere, vmem],
        out_specs=[vmem] * 5,
        scratch_shapes=[
            pltpu.VMEM((rows, cols, channels), BF16),
            pltpu.VMEM((rows, cols, channels), BF16),
            pltpu.VMEM((blocks, 56, channels), F32),
            pltpu.VMEM((blocks, channels, units), BF16),
            pltpu.VMEM((blocks, units, channels), BF16),
            pltpu.VMEM((blocks, chunks, rows, cols + 2 * PAD, LANES), F32),
            pltpu.VMEM((chunks, rows, cols + 2 * PAD, LANES), F32),
            pltpu.VMEM((positions, channels), F32),
            pltpu.VMEM((chunks, positions, LANES), F32),
            pltpu.VMEM((blocks, positions, channels), F32),
            pltpu.VMEM((blocks, positions, LANES), F32),
            pltpu.VMEM((blocks, positions, channels), BF16),
            pltpu.VMEM((blocks, positions, units), BF16),
            pltpu.VMEM((blocks, positions, units), F32),
            pltpu.VMEM((blocks, positions, channels), F32),
            pltpu.VMEM((positions, channels), F32),
            pltpu.VMEM((positions, channels), BF16),
            pltpu.VMEM((positions, units), BF16),
            pltpu.VMEM((2, LANES // 2, channels), F32),
            pltpu.VMEM((blocks, NC, NZ, 2 * span, wide_half), BF16),
            pltpu.VMEM((blocks, NC, NZ, 2 * span, wide_half), BF16),
            pltpu.VMEM((blocks // 2, NC, NZ, span, LANES), F32),
            pltpu.VMEM((blocks, NZ, 2 * span, wide_half), BF16),
            pltpu.VMEM((blocks, NZ, 2 * span, wide_half), BF16),
            pltpu.VMEM((blocks // 2, NZ, span, LANES), F32),
            pltpu.VMEM((blocks, NZ - 1, 2 * span, wide_half), BF16),
            pltpu.VMEM((blocks, NZ - 1, 2 * span, wide_half), BF16),
            pltpu.VMEM((blocks // 2, NZ - 1, span, LANES), F32),
            pltpu.VMEM((2 * span, wide_half), F32),
            pltpu.VMEM((span, LANES), F32),
            pltpu.VMEM((2, blocks // 2, NY, 2, 8, wide_half), F32),
            pltpu.VMEM((blocks // 2, NY, 16, wide_half), BF16),
            pltpu.VMEM((blocks // 2, NY, 16, wide_half), BF16),
            pltpu.VMEM((blocks // 2, NY - 1, 16, wide_half), BF16),
            pltpu.VMEM((blocks // 2, NY - 1, 16, wide_half), BF16),
            pltpu.VMEM((blocks, 8, wide_half), F32),
            pltpu.VMEM((blocks, 8, wide_half), F32),
            pltpu.VMEM((NX - 1, 8, wide_half), F32),
            pltpu.VMEM((NX - 1, 8, wide_half), F32),
            dma((4,)),
            dma((NX - 1,)),
            dma((NX - 1,)),
            dma((3,)),
            dma((NX - 1,)),
            dma((3,)),
            dma((NX - 1,)),
            dma((NX - 1,)),
            dma((NX - 1,)),
            dma((NX - 1,)),
            dma((NX - 1,)),
            dma((blocks, 3)),
            dma((blocks, 3)),
            dma((blocks, 3, NZ - 1)),
            dma((blocks, 3, NZ - 1)),
            dma((blocks, 3)),
            dma((blocks, 3)),
            dma((3,)),
            dma((3,)),
        ],
        compiler_params=pltpu.CompilerParams(
            vmem_limit_bytes=60 * 1024 * 1024, collective_id=0, has_side_effects=True
        ),
        name="blocks",
    )(images, cotangent, kernels.transpose(1, 0, 2), norm_gains, scales, w_in, w_out, orders)
    return (
        grad_kernel.transpose(1, 2, 0),
        grad_gain,
        grad_in.transpose(1, 0, 2),
        grad_out.transpose(1, 2, 0),
        grad_scale,
    )


def solution(mesh):
    in_specs = (
        P("dp", None, None, None),
        P("dp", None, None, None),
        P("segment", None, None),
        P("segment", None),
        P("segment", None, None),
        P("segment", None, None),
        P("segment", None),
    )
    out_specs = (
        P("segment", None, "dp"),
        P("segment", "dp"),
        P("segment", "dp", None),
        P("segment", None, "dp"),
        P("segment", "dp"),
    )
    return jax.shard_map(local, mesh=mesh, in_specs=in_specs, out_specs=out_specs, check_vma=False)
```
